32 devices in a mesh: groups: 2 (over y), gx: 4 (over z), gy: 2 (over x), gz: 2 (over core).
Axes of the slice: x: 2, y: 2, z: 4, core: 2. Of those that a mesh axis runs over, the one named last changes fastest.
Arguments:
- adjoint_one_start: float32 [8, 2, 64, 256], P(('groups', 'gx'), 'gy', 'gz'), parts along dimension 0, may hold values from -6 to 6
- adjoint_two_start: float32 [8, 2, 64, 256], P(('groups', 'gx'), 'gy', 'gz'), parts along dimension 0, may hold values from -6 to 6
- couple_panel: float32 [8, 2, 256, 512], P(('groups', 'gx'), 'gy'), parts along dimension 0, may hold values from -0.21875 to 0.21875
- pair_panel: float32 [8, 2, 512, 256], P(('groups', 'gx'), 'gy'), parts along dimension 0, may hold values from -0.25 to 0.25
- lift_panel: float32 [8, 2, 256, 1024], P(('groups', 'gx'), 'gy'), parts along dimension 0, may hold values from -0.25 to 0.25
- root_panel: float32 [8, 2, 1024, 256], P(('groups', 'gx'), 'gy'), parts along dimension 0, may hold values from -0.125 to 0.125
- back_panel: float32 [8, 2, 1024, 256], P(('groups', 'gx'), 'gy'), parts along dimension 0, may hold values from -0.09375 to 0.09375
- mass_two: float32 [8, 2, 256], P(('groups', 'gx'), 'gy'), parts along dimension 0, may hold values from 0.5 to 1.5
- probe_cells: int32 [128], P(('groups', 'gz')), parts along dimension 0, may hold values from 0 to 2047
- probe_weight: float32 [18, 64], P('groups', 'gz'), parts along dimension 0, may hold values from -48 to 48
Outputs:
- adjoint_one: float32 [8, 2, 64, 256], P(('groups', 'gx'), 'gy', 'gz'), parts along dimension 0
- adjoint_two: float32 [8, 2, 64, 256], P(('groups', 'gx'), 'gy', 'gz'), parts along dimension 0
The draws below stay inside these ranges and needn't reach their ends.
There are 2 independent parts, one for each index of `groups`. The reference program is written for one: setup_inputs(seed, part) draws one part's arguments, and reference() takes and returns one part's arrays. A program takes and returns all parts, laid end to end along the dimension named above; each array names one. Nothing has to cross between parts.
All inputs are finite; a program needn't handle non-finite values.
Results may differ from the reference program's by a relative error of at most 0.00022.
Values sent between devices are 32-bit elements; how exact they have to be, the bound alone decides.
No kernel may reach another device: no remote copies, remote signals or barrier semaphores. Data moves between devices by JAX's collectives and lax.ppermute only.
A program may use at most 64 MiB of HBM per device.

```python
import jax
import jax.numpy as jnp
from jax import lax

R = 64
S = 256
STEPS = 9
TILES_X = 4
TILES_Y = 2


def set_ends(array, rng, low, high):
    longest = array.shape.index(max(array.shape))
    spots = []
    for shift in (0, 1):
        where = [jax.random.randint(jax.random.fold_in(rng, axis), (), 0, length) for axis, length in enumerate(array.shape)]
        where[longest] = (where[longest] + shift) % array.shape[longest]
        spots.append(tuple(where))
    return array.at[spots[0]].set(low).at[spots[1]].set(high)


def level_of(rng, extent, pieces, smallest, high):
    def one(position, parts):
        draws = jax.random.uniform(jax.random.fold_in(jax.random.fold_in(rng, 6), position), (parts,), jnp.float32, smallest / len(pieces), high / len(pieces))
        return jnp.repeat(jnp.exp(draws), extent[position] // parts).reshape((-1,) + (1,) * (len(extent) - position - 1))

    gain = one(*pieces[0])
    for cut in pieces[1:]:
        gain = gain * one(*cut)
    return gain


def normal_values(rng, shape, deviation, limit, pieces=(), dtype=jnp.bfloat16):
    drawn = jax.random.normal(rng, shape, jnp.float32) * deviation
    if len(pieces) > 0:
        drawn = level_of(rng, shape, pieces, -0.22, 0.18) * drawn
    return jnp.clip(drawn, min=-limit, max=limit).astype(dtype)


def setup_inputs(seed: int = 0, part: int = 0) -> dict:
    key_of = jax.random.split(jax.random.key(seed), 11)
    part_keys = jax.random.split(jax.random.fold_in(key_of[10], part), 11)
    return {
        "adjoint_one_start": normal_values(part_keys[0], (TILES_X, TILES_Y, R, S), 1.0, 6.0, ((0, 4), (1, 2), (2, 2)), jnp.float32),
        "adjoint_two_start": normal_values(part_keys[1], (TILES_X, TILES_Y, R, S), 1.0, 6.0, ((0, 4), (1, 2), (2, 2)), jnp.float32),
        "couple_panel": normal_values(part_keys[2], (TILES_X, TILES_Y, S, 2 * S), (3 * S) ** -0.5, 0.21875, ((0, 4), (1, 2)), jnp.float32),
        "pair_panel": normal_values(part_keys[3], (TILES_X, TILES_Y, 2 * S, S), (2 * S) ** -0.5, 0.25, ((0, 4), (1, 2)), jnp.float32),
        "lift_panel": normal_values(part_keys[4], (TILES_X, TILES_Y, S, 4 * S), (2 * S) ** -0.5, 0.25, ((0, 4), (1, 2)), jnp.float32),
        "root_panel": normal_values(part_keys[5], (TILES_X, TILES_Y, 4 * S, S), (8 * S) ** -0.5, 0.125, ((0, 4), (1, 2)), jnp.float32),
        "back_panel": normal_values(part_keys[6], (TILES_X, TILES_Y, 4 * S, S), (16 * S) ** -0.5, 0.09375, ((0, 4), (1, 2)), jnp.float32),
        "mass_two": jnp.clip(0.5 + 1.0 * jax.random.uniform(part_keys[7], (TILES_X, TILES_Y, S), jnp.float32) ** level_of(part_keys[7], (TILES_X, TILES_Y, S), ((0, 4), (1, 2)), -0.2, 0.2), 0.5, 1.5),
        "probe_cells": set_ends(jax.random.randint(part_keys[8], (R,), 0, TILES_X * TILES_Y * S), jax.random.fold_in(part_keys[8], 1), 0, (TILES_X * TILES_Y * S) - 1).astype(jnp.int32),
        "probe_weight": normal_values(part_keys[9], (STEPS, R), 8.0, 48.0, ((1, 2),), jnp.float32),
    }


def spread(block, picks):
    lead = block.shape
    grown = block[:, :, :, None, :] * picks[:, :, None, :, None]
    return grown.reshape(lead[0], lead[1], lead[2], picks.shape[2] * lead[3])


def product(left, right):
    return jnp.einsum("abrs,abst->abrt", left, right, precision=lax.Precision.HIGHEST)


def reference(adjoint_one_start, adjoint_two_start, couple_panel, pair_panel, lift_panel, root_panel, back_panel, mass_two, probe_cells, probe_weight):
    tile_ids = (jnp.arange(TILES_X)[:, None] * TILES_Y + jnp.arange(TILES_Y)[None, :]).astype(jnp.int32)
    cell_ids = jnp.arange(S).astype(jnp.int32)
    targets = tile_ids[:, :, None, None] * S + cell_ids[None, None, None, :]
    probe_mask = (probe_cells[None, None, :, None] == targets).astype(jnp.float32)
    x_bits = (jnp.arange(TILES_X) % 2).astype(jnp.int32)
    y_bits = (jnp.arange(TILES_Y) % 2).astype(jnp.int32)
    x_grid = jnp.broadcast_to(x_bits[:, None], (TILES_X, TILES_Y))
    quarter = 2 * y_bits[None, :] + x_bits[:, None]
    half_picks = (x_grid[:, :, None] == jnp.arange(2)[None, None, :]).astype(jnp.float32)
    quarter_picks = (quarter[:, :, None] == jnp.arange(4)[None, None, :]).astype(jnp.float32)
    adj_one = adjoint_one_start
    adj_two = adjoint_two_start
    for step in range(STEPS):
        source = probe_weight[step][None, None, :, None] * probe_mask
        terms_one = product(adj_one, couple_panel) + spread(source, half_picks)
        pairs = terms_one.reshape(TILES_X // 2, 2, TILES_Y, R, 2 * S)
        sums_one = jnp.broadcast_to(jnp.sum(pairs, axis=1, keepdims=True), pairs.shape).reshape(terms_one.shape)
        half_one = product(sums_one, pair_panel)
        terms_two = product(half_one, lift_panel) + spread(adj_two * mass_two[:, :, None, :], quarter_picks)
        quads = terms_two.reshape(TILES_X // 2, 2, TILES_Y // 2, 2, R, 4 * S)
        sums_two = jnp.broadcast_to(jnp.sum(quads, axis=(1, 3), keepdims=True), quads.shape).reshape(terms_two.shape)
        adj_two = product(sums_two, root_panel)
        blocks = adj_two.reshape(TILES_X // 2, 2, TILES_Y // 2, 2, R, S)
        whole_two = jnp.transpose(blocks, (0, 2, 4, 3, 1, 5)).reshape(TILES_X // 2, TILES_Y // 2, R, 4 * S)
        whole_two = jnp.broadcast_to(whole_two[:, None, :, None], (TILES_X // 2, 2, TILES_Y // 2, 2, R, 4 * S)).reshape(TILES_X, TILES_Y, R, 4 * S)
        adj_one = half_one - product(whole_two, back_panel)
    return (adj_one, adj_two)
```

```python
import jax
import jax.numpy as jnp
from jax import lax
from jax.experimental import pallas as pl
from jax.experimental.pallas import tpu as pltpu
from jax.sharding import PartitionSpec as P

F32 = jnp.float32
BF16 = jnp.bfloat16


def from_partner(value, axis):
    pairs = [(source, source ^ 1) for source in range(lax.axis_size(axis))]
    return lax.ppermute(value, axis, pairs)


def exact_dot(left, right):
    return jnp.dot(left, right, precision=lax.Precision.HIGHEST, preferred_element_type=F32)


def halves_of(value):
    high = value.astype(BF16)
    return high, (value - high.astype(F32)).astype(BF16)


def store_split(high_ref, low_ref, where, value):
    high, low = halves_of(value)
    high_ref[where] = high
    low_ref[where] = low


def tall_kernel(place, own, *refs):
    high_ref, low_ref = refs[6:]
    quarter, core = place[0], place[1]
    half = own.shape[0] // 2
    store_split(high_ref, low_ref, quarter, own[...])
    for tile in range(1, 4):
        for part in range(2):
            rows = pl.ds(pl.multiple_of((core ^ part) * half, half), half)
            store_split(high_ref, low_ref, (quarter ^ tile, rows, slice(None)), refs[2 * (tile - 1) + part][...])


def wide_kernel(place, own, *refs):
    high_ref, low_ref = refs[6:]
    quarter, core = place[0], place[1]
    width = own.shape[0]
    rows = pl.ds(pl.multiple_of(quarter * width, width), width)
    for block in range(4):
        store_split(high_ref, low_ref, (block, rows, slice(None)), own[:, block * width:(block + 1) * width])
    for tile in range(1, 4):
        rows = pl.ds(pl.multiple_of((quarter ^ tile) * width, width), width)
        for part in range(2):
            piece = refs[2 * (tile - 1) + part]
            for block in range(2):
                store_split(
                    high_ref,
                    low_ref,
                    (2 * (core ^ part) + block, rows, slice(None)),
                    piece[:, block * width:(block + 1) * width],
                )


def edge_kernel(place, *refs):
    high_ref, low_ref = refs[8:]
    quarter, core = place[0], place[1]
    rows = refs[0].shape[0] // 2
    for tile in range(4):
        for part in range(2):
            piece = refs[2 * tile + part]
            for bit in range(2):
                start = bit * 2 * rows + (core ^ part) * rows
                store_split(
                    high_ref,
                    low_ref,
                    (quarter ^ tile, pl.ds(pl.multiple_of(start, rows), rows), slice(None)),
                    piece[bit * rows:(bit + 1) * rows, :],
                )


def split_call(kernel, place, shape, arrays):
    out = jax.ShapeDtypeStruct(shape, BF16)
    vmem = pl.BlockSpec(memory_space=pltpu.VMEM)
    return pl.pallas_call(
        kernel,
        in_specs=[pl.BlockSpec(memory_space=pltpu.SMEM)] + [vmem] * len(arrays),
        out_specs=(vmem, vmem),
        out_shape=(out, out),
        compiler_params=pltpu.CompilerParams(vmem_limit_bytes=24 * 2**20),
    )(place, *arrays)


def product(left, high, low):
    rows = left.shape[0]
    left_high, left_low = halves_of(left)
    both = jnp.dot(jnp.concatenate([left_high, left_low], axis=0), high, preferred_element_type=F32)
    rest = jnp.dot(left_high, low, preferred_element_type=F32)
    return both[:rows] + both[rows:] + rest


def march_kernel(place, s0, s1, s2, s3, weight, eh, el, lh, ll, rh, rl, bh, bl, one_ref, two_ref, starts, picks, mass):
    quarter = place[0]
    rows, width = one_ref.shape
    for tile, state in enumerate((s0, s1, s2, s3)):
        where = quarter ^ tile
        starts[0, where] = state[:rows, :width]
        starts[1, where] = state[:rows, width:2 * width]
        picks[where] = state[:rows, 2 * width:]
        mass[where] = state[rows:, :width]
    scale = jnp.concatenate([mass[tile][:1, :] for tile in range(4)], axis=1)
    picked = jnp.concatenate([picks[tile] for tile in range(4)], axis=1)

    def advance(step, carry):
        one, two = carry
        half = jnp.concatenate(
            [product(one[:, (tile // 2) * 2 * width:(tile // 2 + 1) * 2 * width], eh[tile], el[tile]) for tile in range(4)],
            axis=1,
        )
        half = half + weight[step] * picked
        sums = jnp.concatenate([product(half, lh[block], ll[block]) for block in range(4)], axis=1) + two * scale
        two = jnp.concatenate([product(sums, rh[tile], rl[tile]) for tile in range(4)], axis=1)
        back = jnp.concatenate([product(two, bh[tile], bl[tile]) for tile in range(4)], axis=1)
        return half - back, two

    first = tuple(jnp.concatenate([starts[which, tile] for tile in range(4)], axis=1) for which in range(2))
    one, two = lax.fori_loop(0, weight.shape[0], advance, first)
    for tile in range(4):
        starts[0, tile] = one[:, tile * width:(tile + 1) * width]
        starts[1, tile] = two[:, tile * width:(tile + 1) * width]
    one_ref[...] = starts[0, quarter]
    two_ref[...] = starts[1, quarter]


def shards(
    adjoint_one_start,
    adjoint_two_start,
    couple_panel,
    pair_panel,
    lift_panel,
    root_panel,
    back_panel,
    mass_two,
    probe_cells,
    probe_weight,
):
    couple = couple_panel[0, 0]
    pair_cols = pair_panel[0, 0]
    lift = lift_panel[0, 0]
    root = root_panel[0, 0]
    back = back_panel[0, 0]
    mass = mass_two[0, 0]
    width = couple.shape[0]
    rows = probe_cells.shape[0]
    column, row, core = lax.axis_index("gx"), lax.axis_index("gy"), lax.axis_index("gz")
    x_bit, y_bit = column % 2, row % 2
    quarter = 2 * y_bit + x_bit
    place = jnp.stack([quarter, core]).astype(jnp.int32)

    def half_rows(panel):
        size = panel.shape[0] // 2
        return lax.dynamic_slice_in_dim(panel, core * size, size, 0)

    owners = (column - x_bit + jnp.arange(2)) * lax.axis_size("gy") + row
    targets = (owners[:, None] * width + jnp.arange(width)[None, :]).reshape(-1)
    chosen = (probe_cells[:, None] == targets[None, :]).astype(F32)
    picked = exact_dot(chosen, pair_cols)
    state = jnp.concatenate([adjoint_one_start[0, 0], adjoint_two_start[0, 0], picked], axis=1)
    state = jnp.concatenate([state, jnp.broadcast_to(jnp.pad(mass, (0, 2 * width)), (8, 3 * width))], axis=0)

    couple_mine = half_rows(couple)
    couple_other = from_partner(couple_mine, "gx")
    own = {
        "S": state,
        "L": lax.dynamic_slice_in_dim(lift, core * 2 * width, 2 * width, 1),
        "R": half_rows(root),
        "B": half_rows(back),
    }
    first = jnp.where(x_bit == 0, couple_mine, couple_other)
    second = jnp.where(x_bit == 0, couple_other, couple_mine)
    own["E"] = exact_dot(jnp.concatenate([first, second], axis=0), pair_cols)

    across_x = {name: from_partner(own[name], "gx") for name in ("S", "R", "B", "E", "L")}
    across_y = {name: from_partner(own[name], "gy") for name in ("L", "E", "S", "R", "B")}
    diagonal = {name: from_partner(across_y[name], "gx") for name in ("E", "L")}
    diagonal.update({name: from_partner(across_x[name], "gy") for name in ("S", "R", "B")})

    def both(name):
        arrays = []
        for tile in (across_x, across_y, diagonal):
            arrays += [tile[name], from_partner(tile[name], "gz")]
        return arrays

    edge_high, edge_low = split_call(
        edge_kernel, place, (4, 2 * width, width), [own["E"], from_partner(own["E"], "gz")] + both("E")
    )
    lift_high, lift_low = split_call(wide_kernel, place, (4, 4 * width, width), [lift] + both("L"))
    root_high, root_low = split_call(tall_kernel, place, (4, 4 * width, width), [root] + both("R"))
    back_high, back_low = split_call(tall_kernel, place, (4, 4 * width, width), [back] + both("B"))

    vmem = pl.BlockSpec(memory_space=pltpu.VMEM)
    one, two = pl.pallas_call(
        march_kernel,
        in_specs=[pl.BlockSpec(memory_space=pltpu.SMEM)] + [vmem] * 13,
        out_specs=(vmem, vmem),
        out_shape=(jax.ShapeDtypeStruct((rows, width), F32),) * 2,
        scratch_shapes=[
            pltpu.VMEM((2, 4, rows, width), F32),
            pltpu.VMEM((4, rows, width), F32),
            pltpu.VMEM((4, 8, width), F32),
        ],
        compiler_params=pltpu.CompilerParams(vmem_limit_bytes=40 * 2**20),
    )(
        place,
        state,
        across_x["S"],
        across_y["S"],
        diagonal["S"],
        probe_weight[:, :, None],
        edge_high,
        edge_low,
        lift_high,
        lift_low,
        root_high,
        root_low,
        back_high,
        back_low,
    )
    return (one[None, None], two[None, None])


def solution(mesh):
    placed = (
        P(("groups", "gx"), "gy", "gz", None),
        P(("groups", "gx"), "gy", "gz", None),
        P(("groups", "gx"), "gy", None, None),
        P(("groups", "gx"), "gy", None, None),
        P(("groups", "gx"), "gy", None, None),
        P(("groups", "gx"), "gy", None, None),
        P(("groups", "gx"), "gy", None, None),
        P(("groups", "gx"), "gy", None),
        P(("groups", "gz")),
        P("groups", "gz"),
    )
    return jax.shard_map(
        shards,
        mesh=mesh,
        in_specs=placed,
        out_specs=(P(("groups", "gx"), "gy", "gz", None), P(("groups", "gx"), "gy", "gz", None)),
        check_vma=False,
    )
```

```python
import jax
import jax.numpy as jnp
from jax import lax
from jax.experimental import pallas as pl
from jax.experimental.pallas import tpu as pltpu
from jax.sharding import PartitionSpec as P

F32 = jnp.float32
BF16 = jnp.bfloat16


def from_partner(value, axis):
    pairs = [(source, source ^ 1) for source in range(lax.axis_size(axis))]
    return lax.ppermute(value, axis, pairs)


def after(value, *earlier):
    return lax.optimization_barrier((value,) + earlier)[0]


def exact_dot(left, right):
    return jnp.dot(left, right, precision=lax.Precision.HIGHEST, preferred_element_type=F32)


def halves_of(value):
    high = value.astype(BF16)
    return high, (value - high.astype(F32)).astype(BF16)


def store_split(high_ref, low_ref, where, value):
    high, low = halves_of(value)
    high_ref[where] = high
    low_ref[where] = low


def start_copies(sources, targets, sems):
    copies = [pltpu.make_async_copy(source, target, sems.at[i]) for i, (source, target) in enumerate(zip(sources, targets))]
    for copy in copies:
        copy.start()
    return copies


def split_tall_half(place, part, piece, high_ref, low_ref, lead):
    width = piece.shape[1]
    for block in range(2):
        target = (2 * (place[1] ^ part) + block) ^ place[0]
        rows = pl.ds(pl.multiple_of(target * width, width), width)
        store_split(high_ref, low_ref, lead + (rows, slice(None)), piece[block * width:(block + 1) * width, :])


def tall_kernel(place, own, *refs):
    pieces, (high_ref, low_ref, whole, halves, sems) = refs[:4], refs[4:]
    copies = start_copies((own,) + pieces, [whole] + [halves.at[i] for i in range(4)], sems)
    width = whole.shape[1]
    copies[0].wait()
    for block in range(4):
        rows = pl.ds(pl.multiple_of((block ^ place[0]) * width, width), width)
        store_split(high_ref, low_ref, (0, rows, slice(None)), whole[block * width:(block + 1) * width, :])
    for index in range(4):
        copies[1 + index].wait()
        split_tall_half(place, index % 2, halves.at[index], high_ref, low_ref, (1 + index // 2,))


def wide_kernel(place, own, *refs):
    pieces, (high_ref, low_ref, whole, halves, sems) = refs[:6], refs[6:]
    copies = start_copies((own,) + pieces, [whole] + [halves.at[i] for i in range(6)], sems)
    width = whole.shape[0]
    copies[0].wait()
    for block in range(4):
        store_split(
            high_ref, low_ref, (block ^ place[0], slice(0, width), slice(None)), whole[:, block * width:(block + 1) * width]
        )
    for index in range(6):
        copies[1 + index].wait()
        tile, part = 1 + index // 2, index % 2
        for block in range(2):
            store_split(
                high_ref,
                low_ref,
                ((2 * (place[1] ^ part) + block) ^ place[0], slice(tile * width, (tile + 1) * width), slice(None)),
                halves[index, :, block * width:(block + 1) * width],
            )


def edge_kernel(place, *refs):
    pieces, (high_ref, low_ref, halves, sems) = refs[:8], refs[8:]
    copies = start_copies(pieces, [halves.at[i] for i in range(8)], sems)
    rows = halves.shape[1] // 2
    for index in range(8):
        copies[index].wait()
        for bit in range(2):
            start = (bit ^ (place[0] % 2)) * 2 * rows + (place[1] ^ (index % 2)) * rows
            store_split(
                high_ref,
                low_ref,
                (index // 2, pl.ds(pl.multiple_of(start, rows), rows), slice(None)),
                halves[index, bit * rows:(bit + 1) * rows, :],
            )


def split_call(kernel, place, shape, arrays, scratch):
    out = jax.ShapeDtypeStruct(shape, BF16)
    vmem = pl.BlockSpec(memory_space=pltpu.VMEM)
    return pl.pallas_call(
        kernel,
        in_specs=[pl.BlockSpec(memory_space=pltpu.SMEM)] + [pl.BlockSpec(memory_space=pltpu.HBM)] * len(arrays),
        out_specs=(vmem, vmem),
        out_shape=(out, out),
        scratch_shapes=[pltpu.VMEM(size, F32) for size in scratch] + [pltpu.SemaphoreType.DMA((len(arrays),))],
        compiler_params=pltpu.CompilerParams(vmem_limit_bytes=14 * 2**20),
    )(place, *arrays)


def product(left, high, low):
    rows = left.shape[0]
    left_high, left_low = halves_of(left)
    both = jnp.dot(jnp.concatenate([left_high, left_low], axis=0), high, preferred_element_type=F32)
    rest = jnp.dot(left_high, low, preferred_element_type=F32)
    return both[:rows] + both[rows:] + rest


def march_kernel(place, s0, s1, s2, s3, weight, eh, el, lh, ll, rh, rl, bh, bl, r_mine, r_other, b_mine, b_other, *refs):
    one_ref, two_ref, last_rh, last_rl, last_bh, last_bl, halves, sems = refs
    rows, width = one_ref.shape
    copies = start_copies((r_mine, r_other, b_mine, b_other), [halves.at[i] for i in range(4)], sems)
    states = (s0, s1, s2, s3)
    one = jnp.concatenate([state[:rows, :width] for state in states], axis=1)
    two = jnp.concatenate([state[:rows, width:2 * width] for state in states], axis=1)
    picked = jnp.concatenate([state[:rows, 2 * width:] for state in states], axis=1)
    scale = jnp.concatenate([state[rows:rows + 1, :width] for state in states], axis=1)
    for index in range(4):
        copies[index].wait()
        high_ref, low_ref = ((last_rh, last_rl), (last_bh, last_bl))[index // 2]
        split_tall_half(place, index % 2, halves.at[index], high_ref, low_ref, ())

    def tall(left, high, low, last_high, last_low):
        blocks = [product(left, high[tile], low[tile]) for tile in range(3)]
        return jnp.concatenate(blocks + [product(left, last_high[...], last_low[...])], axis=1)

    def advance(step, carry):
        one, two = carry
        half = jnp.concatenate(
            [product(one[:, (tile // 2) * 2 * width:(tile // 2 + 1) * 2 * width], eh[tile], el[tile]) for tile in range(4)],
            axis=1,
        )
        half = half + weight[step] * picked
        sums = jnp.concatenate([product(half, lh[block], ll[block]) for block in range(4)], axis=1) + two * scale
        two = tall(sums, rh, rl, last_rh, last_rl)
        return half - tall(two, bh, bl, last_bh, last_bl), two

    one, two = lax.fori_loop(0, weight.shape[0], advance, (one, two))
    one_ref[...] = one[:, :width]
    two_ref[...] = two[:, :width]


def shards(
    adjoint_one_start,
    adjoint_two_start,
    couple_panel,
    pair_panel,
    lift_panel,
    root_panel,
    back_panel,
    mass_two,
    probe_cells,
    probe_weight,
):
    couple = couple_panel[0, 0]
    pair_cols = pair_panel[0, 0]
    lift = lift_panel[0, 0]
    root = root_panel[0, 0]
    back = back_panel[0, 0]
    mass = mass_two[0, 0]
    width = couple.shape[0]
    rows = probe_cells.shape[0]
    column, row, core = lax.axis_index("gx"), lax.axis_index("gy"), lax.axis_index("gz")
    x_bit, y_bit = column % 2, row % 2
    place = jnp.stack([2 * y_bit + x_bit, core]).astype(jnp.int32)

    def half_rows(panel):
        size = panel.shape[0] // 2
        return lax.dynamic_slice_in_dim(panel, core * size, size, 0)

    owners = (column - x_bit + jnp.arange(2)) * lax.axis_size("gy") + row
    targets = (owners[:, None] * width + jnp.arange(width)[None, :]).reshape(-1)
    chosen = (probe_cells[:, None] == targets[None, :]).astype(F32)
    picked = exact_dot(chosen, pair_cols)
    state = jnp.concatenate([adjoint_one_start[0, 0], adjoint_two_start[0, 0], picked], axis=1)
    state = jnp.concatenate([state, jnp.broadcast_to(jnp.pad(mass, (0, 2 * width)), (8, 3 * width))], axis=0)
    lift_half = lax.dynamic_slice_in_dim(lift, core * 2 * width, 2 * width, 1)
    root_half = half_rows(root)
    back_half = half_rows(back)

    couple_mine = half_rows(couple)
    couple_other = from_partner(couple_mine, "gx")
    state_x = from_partner(state, "gx")
    state_y = from_partner(state, "gy")
    lift_y = from_partner(lift_half, "gy")

    first = jnp.where(x_bit == 0, couple_mine, couple_other)
    second = jnp.where(x_bit == 0, couple_other, couple_mine)
    edge_half = exact_dot(jnp.concatenate([first, second], axis=0), pair_cols)

    lift_x = from_partner(after(lift_half, couple_other), "gx")
    back_y = from_partner(after(back_half, state_y), "gy")
    root_x = from_partner(after(root_half, state_x), "gx")
    edge_y = from_partner(after(edge_half, lift_y), "gy")
    back_x = from_partner(after(back_half, lift_x), "gx")
    root_y = from_partner(after(root_half, back_y), "gy")
    edge_x = from_partner(after(edge_half, root_x), "gx")
    state_d = from_partner(after(state_x, edge_y), "gy")
    lift_d = from_partner(after(lift_x, root_y), "gy")
    edge_d = from_partner(after(edge_y, back_x), "gx")
    back_d = from_partner(after(back_y, edge_x), "gx")
    root_d = from_partner(after(root_x, state_d), "gy")

    def both(*values):
        arrays = []
        for value in values:
            arrays += [value, from_partner(value, "gz")]
        return arrays

    tall_scratch = [(4 * width, width), (4, 2 * width, width)]
    back_high, back_low = split_call(tall_kernel, place, (3, 4 * width, width), [back] + both(back_x, back_y), tall_scratch)
    root_high, root_low = split_call(tall_kernel, place, (3, 4 * width, width), [root] + both(root_x, root_y), tall_scratch)
    edge_high, edge_low = split_call(
        edge_kernel, place, (4, 2 * width, width), both(edge_half, edge_x, edge_y, edge_d), [(8, width, width)]
    )
    lift_high, lift_low = split_call(
        wide_kernel, place, (4, 4 * width, width), [lift] + both(lift_x, lift_y, lift_d), [(width, 4 * width), (6, width, 2 * width)]
    )

    vmem = pl.BlockSpec(memory_space=pltpu.VMEM)
    one, two = pl.pallas_call(
        march_kernel,
        in_specs=[pl.BlockSpec(memory_space=pltpu.SMEM)] + [vmem] * 13 + [pl.BlockSpec(memory_space=pltpu.HBM)] * 4,
        out_specs=(vmem, vmem),
        out_shape=(jax.ShapeDtypeStruct((rows, width), F32),) * 2,
        scratch_shapes=[pltpu.VMEM((4 * width, width), BF16)] * 4
        + [pltpu.VMEM((4, 2 * width, width), F32), pltpu.SemaphoreType.DMA((4,))],
        compiler_params=pltpu.CompilerParams(vmem_limit_bytes=14 * 2**20),
    )(
        place,
        state,
        state_x,
        state_y,
        state_d,
        probe_weight[:, :, None],
        edge_high,
        edge_low,
        lift_high,
        lift_low,
        root_high,
        root_low,
        back_high,
        back_low,
        *both(root_d, back_d),
    )
    return (one[None, None], two[None, None])


def solution(mesh):
    placed = (
        P(("groups", "gx"), "gy", "gz", None),
        P(("groups", "gx"), "gy", "gz", None),
        P(("groups", "gx"), "gy", None, None),
        P(("groups", "gx"), "gy", None, None),
        P(("groups", "gx"), "gy", None, None),
        P(("groups", "gx"), "gy", None, None),
        P(("groups", "gx"), "gy", None, None),
        P(("groups", "gx"), "gy", None),
        P(("groups", "gz")),
        P("groups", "gz"),
    )
    return jax.shard_map(
        shards,
        mesh=mesh,
        in_specs=placed,
        out_specs=(P(("groups", "gx"), "gy", "gz", None), P(("groups", "gx"), "gy", "gz", None)),
        check_vma=False,
    )
```

```python
import jax
import jax.numpy as jnp
from jax import lax
from jax.experimental import pallas as pl
from jax.experimental.pallas import tpu as pltpu
from jax.sharding import PartitionSpec as P

F32 = jnp.float32
BF16 = jnp.bfloat16


def from_partner(value, axis):
    pairs = [(source, source ^ 1) for source in range(lax.axis_size(axis))]
    return lax.ppermute(value, axis, pairs)


def after(value, *earlier):
    return lax.optimization_barrier((value,) + earlier)[0]


def exact_dot(left, right):
    return jnp.dot(left, right, precision=lax.Precision.HIGHEST, preferred_element_type=F32)


def halves_of(value):
    high = value.astype(BF16)
    return high, (value - high.astype(F32)).astype(BF16)


def store_split(high_ref, low_ref, where, value):
    high, low = halves_of(value)
    high_ref[where] = high
    low_ref[where] = low


def cut_kernel(place, *refs):
    count = (len(refs) - 1) // 2
    panels, halves, sems = refs[:count], refs[count:2 * count], refs[-1]
    copies = []
    for index, (panel, half) in enumerate(zip(panels, halves)):
        rows, columns = half.shape
        if columns < panel.shape[1]:
            source = panel.at[:, pl.ds(pl.multiple_of(place[1] * columns, columns), columns)]
        else:
            source = panel.at[pl.ds(pl.multiple_of(place[1] * rows, rows), rows), :]
        copies.append(pltpu.make_async_copy(source, half, sems.at[index]))
    for copy in copies:
        copy.start()
    for copy in copies:
        copy.wait()


def cut_call(place, panels, shapes):
    hbm = [pltpu.with_memory_space_constraint(panel, pltpu.HBM) for panel in panels]
    return pl.pallas_call(
        cut_kernel,
        in_specs=[pl.BlockSpec(memory_space=pltpu.SMEM)] + [pl.BlockSpec(memory_space=pl.ANY)] * len(panels),
        out_specs=[pl.BlockSpec(memory_space=pl.ANY)] * len(panels),
        out_shape=[jax.ShapeDtypeStruct(shape, F32) for shape in shapes],
        scratch_shapes=[pltpu.SemaphoreType.DMA((len(panels),))],
        compiler_params=pltpu.CompilerParams(vmem_limit_bytes=2**20),
    )(place, *hbm)


def column_of(row):
    shape = (row.shape[1], row.shape[1])
    same = lax.broadcasted_iota(jnp.int32, shape, 0) == lax.broadcasted_iota(jnp.int32, shape, 1)
    return jnp.sum(jnp.where(same, row, 0.0), axis=1, keepdims=True)


def state_kernel(place, cells, one, two, pair_cols, mass, state_ref):
    rows, width = one.shape
    cell = column_of(cells[...].astype(F32))
    number = lax.broadcasted_iota(jnp.int32, (rows, width), 1)
    chosen = [(cell == (number + place[2 + side]).astype(F32)).astype(F32) for side in range(2)]
    state_ref[:rows, :width] = one[...]
    state_ref[:rows, width:2 * width] = two[...]
    state_ref[:rows, 2 * width:] = exact_dot(jnp.concatenate(chosen, axis=1), pair_cols[...])
    state_ref[rows:, :width] = jnp.broadcast_to(mass[...], (8, width))
    state_ref[rows:, width:] = jnp.zeros((8, 2 * width), F32)


def panel_kernel(place, mine, other, pair_cols, panel_ref):
    rows = mine.shape[0]
    for step, couple in enumerate((mine, other)):
        start = ((place[0] % 2) ^ step) * rows
        panel_ref[pl.ds(pl.multiple_of(start, rows), rows), :] = exact_dot(couple[...], pair_cols[...])


def small_call(kernel, shape, *values):
    vmem = pl.BlockSpec(memory_space=pltpu.VMEM)
    return pl.pallas_call(
        kernel,
        in_specs=[pl.BlockSpec(memory_space=pltpu.SMEM)] + [vmem] * (len(values) - 1),
        out_specs=vmem,
        out_shape=jax.ShapeDtypeStruct(shape, F32),
        compiler_params=pltpu.CompilerParams(vmem_limit_bytes=6 * 2**20),
    )(*values)


def split_tall(place, pieces, high_ref, low_ref):
    width = high_ref.shape[1]
    blocks = 4 // len(pieces)
    for part, piece in enumerate(pieces):
        for block in range(blocks):
            number = block if len(pieces) == 1 else 2 * (place[1] ^ part) + block
            rows = pl.ds(pl.multiple_of((number ^ place[0]) * width, width), width)
            store_split(high_ref, low_ref, (rows, slice(None)), piece[block * width:(block + 1) * width, :])


def tall_kernel(place, *refs):
    split_tall(place, refs[:-2], *refs[-2:])


def wide_kernel(place, *refs):
    pieces, (high_ref, low_ref) = refs[:-2], refs[-2:]
    width = high_ref.shape[1]
    blocks = 4 // len(pieces)
    for part, piece in enumerate(pieces):
        for block in range(blocks):
            number = block if len(pieces) == 1 else 2 * (place[1] ^ part) + block
            rows = pl.ds(pl.multiple_of((number ^ place[0]) * width, width), width)
            store_split(high_ref, low_ref, (rows, slice(None)), piece[:, block * width:(block + 1) * width])


def edge_kernel(place, *refs):
    pieces, (high_ref, low_ref) = refs[:-2], refs[-2:]
    rows = pieces[0].shape[0] // 2
    for part, piece in enumerate(pieces):
        for bit in range(2):
            start = (bit ^ (place[0] % 2)) * 2 * rows + (place[1] ^ part) * rows
            where = (pl.ds(pl.multiple_of(start, rows), rows), slice(None))
            store_split(high_ref, low_ref, where, piece[bit * rows:(bit + 1) * rows, :])


def split_call(kernel, place, rows, *pieces):
    out = jax.ShapeDtypeStruct((rows, pieces[0].shape[1]), BF16)
    if kernel is wide_kernel:
        out = jax.ShapeDtypeStruct((rows, pieces[0].shape[0]), BF16)
    vmem = pl.BlockSpec(memory_space=pltpu.VMEM)
    return pl.pallas_call(
        kernel,
        in_specs=[pl.BlockSpec(memory_space=pltpu.SMEM)] + [vmem] * len(pieces),
        out_specs=(vmem, vmem),
        out_shape=(pltpu.VMEM(out.shape, BF16),) * 2,
        compiler_params=pltpu.CompilerParams(vmem_limit_bytes=4 * 2**20),
    )(place, *pieces)


def product(left, high, low):
    rows = left.shape[0]
    left_high, left_low = halves_of(left)
    both = jnp.dot(jnp.concatenate([left_high, left_low], axis=0), high, preferred_element_type=F32)
    rest = jnp.dot(left_high, low, preferred_element_type=F32)
    return both[:rows] + both[rows:] + rest


def march_kernel(place, s0, s1, s2, s3, weight, *refs):
    edge, lift, root, back = refs[:8], refs[8:16], refs[16:22], refs[22:28]
    r_mine, r_other, b_mine, b_other, one_ref, two_ref, last_rh, last_rl, last_bh, last_bl = refs[28:]
    rows, width = one_ref.shape
    states = (s0, s1, s2, s3)
    one = jnp.concatenate([state[:rows, :width] for state in states], axis=1)
    two = jnp.concatenate([state[:rows, width:2 * width] for state in states], axis=1)
    picked = jnp.concatenate([state[:rows, 2 * width:] for state in states], axis=1)
    scale = jnp.concatenate([state[rows:rows + 1, :width] for state in states], axis=1)
    split_tall(place, (r_mine, r_other), last_rh, last_rl)
    split_tall(place, (b_mine, b_other), last_bh, last_bl)
    root = root + (last_rh, last_rl)
    back = back + (last_bh, last_bl)

    def tall(left, panels):
        return jnp.concatenate([product(left, panels[2 * tile][...], panels[2 * tile + 1][...]) for tile in range(4)], axis=1)

    def column_block(block, part):
        return jnp.concatenate([lift[2 * tile + part][block * width:(block + 1) * width, :] for tile in range(4)], axis=0)

    def advance(step, carry):
        one, two = carry
        half = jnp.concatenate(
            [
                product(one[:, side * 2 * width:(side + 1) * 2 * width], edge[2 * tile][...], edge[2 * tile + 1][...])
                for side in range(2)
                for tile in (2 * side, 2 * side + 1)
            ],
            axis=1,
        )
        half = half + column_of(weight[pl.ds(step, 1), :]) * picked
        sums = jnp.concatenate([product(half, column_block(block, 0), column_block(block, 1)) for block in range(4)], axis=1)
        two = tall(sums + two * scale, root)
        return half - tall(two, back), two

    one, two = lax.fori_loop(0, weight.shape[0], advance, (one, two))
    one_ref[...] = one[:, :width]
    two_ref[...] = two[:, :width]


def shards(
    adjoint_one_start,
    adjoint_two_start,
    couple_panel,
    pair_panel,
    lift_panel,
    root_panel,
    back_panel,
    mass_two,
    probe_cells,
    probe_weight,
):
    couple = couple_panel[0, 0]
    pair_cols = pair_panel[0, 0]
    lift = lift_panel[0, 0]
    root = root_panel[0, 0]
    back = back_panel[0, 0]
    width = couple.shape[0]
    rows = probe_cells.shape[0]
    column, row, core = lax.axis_index("gx"), lax.axis_index("gy"), lax.axis_index("gz")
    x_bit, y_bit = column % 2, row % 2
    first_cell = ((column - x_bit) * lax.axis_size("gy") + row) * width
    place = jnp.stack([2 * y_bit + x_bit, core, first_cell, first_cell + lax.axis_size("gy") * width]).astype(jnp.int32)

    couple_mine, lift_half = cut_call(place, (couple, lift), ((width // 2, 2 * width), (width, 2 * width)))
    couple_other = from_partner(couple_mine, "gx")
    lift_y = from_partner(lift_half, "gy")
    root_half, back_half = cut_call(after(place, lift_half), (root, back), ((2 * width, width),) * 2)
    lift_x = from_partner(lift_half, "gx")
    back_y = from_partner(back_half, "gy")

    cells = probe_cells[None, :]
    state = small_call(
        state_kernel,
        (rows + 8, 3 * width),
        after(place, root_half),
        cells,
        adjoint_one_start[0, 0],
        adjoint_two_start[0, 0],
        pair_cols,
        mass_two[0],
    )
    edge_half = small_call(panel_kernel, (width, width), place, couple_mine, couple_other, pair_cols)

    token = [couple_other]

    def arrive(value, *done):
        value = after(value, token[0], *done)
        token[0] = value
        return value

    def send(value, axis):
        return from_partner(after(value, token[0]), axis)

    def split(kernel, rows, value):
        return split_call(kernel, place, rows, value, from_partner(value, "gz"))

    tall, wide, edge = (tall_kernel, 4 * width), (wide_kernel, 4 * width), (edge_kernel, 2 * width)
    lift_own = split_call(wide_kernel, place, wide[1], after(lift, couple_other))
    root_own = split_call(tall_kernel, place, tall[1], after(root, couple_other))
    back_own = split_call(tall_kernel, place, tall[1], after(back, couple_other))

    state_x = send(state, "gx")
    root_x = send(root_half, "gx")
    lift_y = arrive(lift_y, lift_own[0], root_own[0], back_own[0])
    edge_own = split(*edge, edge_half)
    edge_y = send(edge_half, "gy")
    state_y = send(state, "gy")
    lift_x = arrive(lift_x, edge_own[0])
    lift_y_split = split(*wide, lift_y)
    back_x = send(back_half, "gx")
    back_y = arrive(back_y, lift_y_split[0])
    lift_x_split = split(*wide, lift_x)
    root_y = send(root_half, "gy")
    edge_y = arrive(edge_y, lift_x_split[0])
    back_y_split = split(*tall, back_y)
    root_x = arrive(root_x, back_y_split[0])
    edge_y_split = split(*edge, edge_y)
    edge_x = send(edge_half, "gx")
    state_y = arrive(state_y)
    state_d = send(state_x, "gy")
    back_x = arrive(back_x, edge_y_split[0])
    root_x_split = split(*tall, root_x)
    edge_d = send(edge_y, "gx")
    root_y = arrive(root_y, root_x_split[0])
    lift_d = send(lift_x, "gy")
    back_x_split = split(*tall, back_x)
    state_d = arrive(state_d)
    root_d = send(root_x, "gy")
    edge_x = arrive(edge_x, back_x_split[0])
    root_y_split = split(*tall, root_y)
    back_d = send(back_y, "gx")
    edge_d = arrive(edge_d, root_y_split[0])
    edge_x_split = split(*edge, edge_x)
    lift_d = arrive(lift_d, edge_x_split[0])
    edge_d_split = split(*edge, edge_d)
    back_d = arrive(back_d, edge_d_split[0])
    lift_d_split = split(*wide, lift_d)
    root_d = arrive(root_d, lift_d_split[0])

    vmem = pl.BlockSpec(memory_space=pltpu.VMEM)
    panels = edge_own + edge_x_split + edge_y_split + edge_d_split + lift_own + lift_x_split + lift_y_split + lift_d_split
    panels += root_own + root_x_split + root_y_split + back_own + back_x_split + back_y_split
    panels = tuple(pltpu.with_memory_space_constraint(panel, pltpu.VMEM) for panel in panels)
    panels += (root_d, from_partner(root_d, "gz"), back_d, from_partner(back_d, "gz"))
    one, two = pl.pallas_call(
        march_kernel,
        in_specs=[pl.BlockSpec(memory_space=pltpu.SMEM)] + [vmem] * (5 + len(panels)),
        out_specs=(vmem, vmem),
        out_shape=(jax.ShapeDtypeStruct((rows, width), F32),) * 2,
        scratch_shapes=[pltpu.VMEM((4 * width, width), BF16)] * 4,
        compiler_params=pltpu.CompilerParams(vmem_limit_bytes=12 * 2**20),
    )(place, state, state_x, state_y, state_d, probe_weight, *panels)
    return (one[None, None], two[None, None])


def solution(mesh):
    placed = (
        P(("groups", "gx"), "gy", "gz", None),
        P(("groups", "gx"), "gy", "gz", None),
        P(("groups", "gx"), "gy", None, None),
        P(("groups", "gx"), "gy", None, None),
        P(("groups", "gx"), "gy", None, None),
        P(("groups", "gx"), "gy", None, None),
        P(("groups", "gx"), "gy", None, None),
        P(("groups", "gx"), "gy", None),
        P(("groups", "gz")),
        P("groups", "gz"),
    )
    return jax.shard_map(
        shards,
        mesh=mesh,
        in_specs=placed,
        out_specs=(P(("groups", "gx"), "gy", "gz", None), P(("groups", "gx"), "gy", "gz", None)),
        check_vma=False,
    )
```

```python
import jax
import jax.numpy as jnp
from jax import lax
from jax.experimental import pallas as pl
from jax.experimental.pallas import tpu as pltpu
from jax.sharding import PartitionSpec as P

F32 = jnp.float32
BF16 = jnp.bfloat16


def from_partner(value, axis):
    pairs = [(source, source ^ 1) for source in range(lax.axis_size(axis))]
    return lax.ppermute(value, axis, pairs)


def after(value, *earlier):
    return lax.optimization_barrier((value,) + earlier)[0]


def exact_dot(left, right):
    return jnp.dot(left, right, precision=lax.Precision.HIGHEST, preferred_element_type=F32)


def halves_of(value):
    high = value.astype(BF16)
    return high, (value - high.astype(F32)).astype(BF16)


def store_split(high_ref, low_ref, where, value):
    high, low = halves_of(value)
    high_ref[where] = high
    low_ref[where] = low


CHEAP = pl.CostEstimate(flops=1, transcendentals=0, bytes_accessed=1)


def cut_kernel(place, *refs):
    count = (len(refs) - 1) // 2
    panels, halves, sems = refs[:count], refs[count:2 * count], refs[-1]
    copies = []
    for index, (panel, half) in enumerate(zip(panels, halves)):
        rows, columns = half.shape
        if columns < panel.shape[1]:
            source = panel.at[:, pl.ds(pl.multiple_of(place[1] * columns, columns), columns)]
        else:
            source = panel.at[pl.ds(pl.multiple_of(place[1] * rows, rows), rows), :]
        copies.append(pltpu.make_async_copy(source, half, sems.at[index]))
    for copy in copies:
        copy.start()
    for copy in copies:
        copy.wait()


def cut_call(place, panels, shapes):
    hbm = [pltpu.with_memory_space_constraint(panel, pltpu.HBM) for panel in panels]
    return pl.pallas_call(
        cut_kernel,
        in_specs=[pl.BlockSpec(memory_space=pltpu.SMEM)] + [pl.BlockSpec(memory_space=pl.ANY)] * len(panels),
        out_specs=[pl.BlockSpec(memory_space=pl.ANY)] * len(panels),
        out_shape=[jax.ShapeDtypeStruct(shape, F32) for shape in shapes],
        scratch_shapes=[pltpu.SemaphoreType.DMA((len(panels),))],
        cost_estimate=CHEAP,
        compiler_params=pltpu.CompilerParams(vmem_limit_bytes=2**20),
    )(place, *hbm)


def column_of(row):
    shape = (row.shape[1], row.shape[1])
    same = lax.broadcasted_iota(jnp.int32, shape, 0) == lax.broadcasted_iota(jnp.int32, shape, 1)
    return jnp.sum(jnp.where(same, row, 0.0), axis=1, keepdims=True)


def edge_state_kernel(place, mine, other, pair_cols, cells, one, two, mass, edge_ref):
    half = mine.shape[0]
    rows, width = one.shape
    for step, couple in enumerate((mine, other)):
        start = ((place[0] % 2) ^ step) * half
        edge_ref[pl.ds(pl.multiple_of(start, half), half), :] = exact_dot(couple[...], pair_cols[...])
    cell = column_of(cells[...].astype(F32))
    number = lax.broadcasted_iota(jnp.int32, (rows, width), 1)
    chosen = [(cell == (number + place[2 + side]).astype(F32)).astype(F32) for side in range(2)]
    picked = exact_dot(jnp.concatenate(chosen, axis=1), pair_cols[...])
    for index, value in enumerate((one[...], two[...], picked)):
        edge_ref[2 * half + index * rows:2 * half + (index + 1) * rows, :] = value
    edge_ref[2 * half + 3 * rows:, :] = jnp.broadcast_to(mass[...], (8, width))


def small_call(kernel, shape, *values):
    vmem = pl.BlockSpec(memory_space=pltpu.VMEM)
    return pl.pallas_call(
        kernel,
        in_specs=[pl.BlockSpec(memory_space=pltpu.SMEM)] + [vmem] * (len(values) - 1),
        out_specs=vmem,
        out_shape=jax.ShapeDtypeStruct(shape, F32),
        cost_estimate=CHEAP,
        compiler_params=pltpu.CompilerParams(vmem_limit_bytes=6 * 2**20),
    )(*values)


def split_tall(place, pieces, high_ref, low_ref):
    width = high_ref.shape[1]
    blocks = 4 // len(pieces)
    for part, piece in enumerate(pieces):
        for block in range(blocks):
            number = block if len(pieces) == 1 else 2 * (place[1] ^ part) + block
            rows = pl.ds(pl.multiple_of((number ^ place[0]) * width, width), width)
            store_split(high_ref, low_ref, (rows, slice(None)), piece[block * width:(block + 1) * width, :])


def tall_kernel(place, *refs):
    split_tall(place, refs[:-2], *refs[-2:])


def wide_kernel(place, *refs):
    pieces, (high_ref, low_ref) = refs[:-2], refs[-2:]
    width = high_ref.shape[1]
    blocks = 4 // len(pieces)
    for part, piece in enumerate(pieces):
        for block in range(blocks):
            number = block if len(pieces) == 1 else 2 * (place[1] ^ part) + block
            rows = pl.ds(pl.multiple_of((number ^ place[0]) * width, width), width)
            store_split(high_ref, low_ref, (rows, slice(None)), piece[:, block * width:(block + 1) * width])


def edge_kernel(place, *refs):
    pieces, (high_ref, low_ref) = refs[:-2], refs[-2:]
    rows = pieces[0].shape[1] // 2
    for part, piece in enumerate(pieces):
        for bit in range(2):
            start = (bit ^ (place[0] % 2)) * 2 * rows + (place[1] ^ part) * rows
            where = (pl.ds(pl.multiple_of(start, rows), rows), slice(None))
            store_split(high_ref, low_ref, where, piece[bit * rows:(bit + 1) * rows, :])


def split_call(kernel, place, rows, *pieces):
    out = jax.ShapeDtypeStruct((rows, pieces[0].shape[1]), BF16)
    if kernel is wide_kernel:
        out = jax.ShapeDtypeStruct((rows, pieces[0].shape[0]), BF16)
    vmem = pl.BlockSpec(memory_space=pltpu.VMEM)
    return pl.pallas_call(
        kernel,
        in_specs=[pl.BlockSpec(memory_space=pltpu.SMEM)] + [vmem] * len(pieces),
        out_specs=(vmem, vmem),
        out_shape=(pltpu.VMEM(out.shape, BF16),) * 2,
        cost_estimate=CHEAP,
        compiler_params=pltpu.CompilerParams(vmem_limit_bytes=4 * 2**20),
    )(place, *pieces)


def product(left, high, low):
    rows = left.shape[0]
    left_high, left_low = halves_of(left)
    both = jnp.dot(jnp.concatenate([left_high, left_low], axis=0), high, preferred_element_type=F32)
    rest = jnp.dot(left_high, low, preferred_element_type=F32)
    return both[:rows] + both[rows:] + rest


def march_kernel(s0, s1, s2, s3, weight, place, *refs):
    edge, lift, root, back = refs[:8], refs[8:16], refs[16:22], refs[22:28]
    r_mine, r_other, b_mine, b_other, one_ref, two_ref, last_rh, last_rl, last_bh, last_bl = refs[28:]
    rows, width = one_ref.shape

    def below(index, count):
        start = width + index * rows
        return jnp.concatenate([tile[start:start + count, :] for tile in (s0, s1, s2, s3)], axis=1)

    one, two, picked, scale = below(0, rows), below(1, rows), below(2, rows), below(3, 1)
    split_tall(place, (r_mine, r_other), last_rh, last_rl)
    split_tall(place, (b_mine, b_other), last_bh, last_bl)
    root = root + (last_rh, last_rl)
    back = back + (last_bh, last_bl)

    def tall(left, panels):
        return jnp.concatenate([product(left, panels[2 * tile][...], panels[2 * tile + 1][...]) for tile in range(4)], axis=1)

    def column_block(block, part):
        return jnp.concatenate([lift[2 * tile + part][block * width:(block + 1) * width, :] for tile in range(4)], axis=0)

    def advance(step, carry):
        one, two = carry
        half = jnp.concatenate(
            [
                product(one[:, side * 2 * width:(side + 1) * 2 * width], edge[2 * tile][...], edge[2 * tile + 1][...])
                for side in range(2)
                for tile in (2 * side, 2 * side + 1)
            ],
            axis=1,
        )
        half = half + column_of(weight[pl.ds(step, 1), :]) * picked
        sums = jnp.concatenate([product(half, column_block(block, 0), column_block(block, 1)) for block in range(4)], axis=1)
        two = tall(sums + two * scale, root)
        return half - tall(two, back), two

    one, two = lax.fori_loop(0, weight.shape[0], advance, (one, two))
    one_ref[...] = one[:, :width]
    two_ref[...] = two[:, :width]


def shards(
    adjoint_one_start,
    adjoint_two_start,
    couple_panel,
    pair_panel,
    lift_panel,
    root_panel,
    back_panel,
    mass_two,
    probe_cells,
    probe_weight,
):
    couple = couple_panel[0, 0]
    pair_cols = pair_panel[0, 0]
    lift = lift_panel[0, 0]
    root = root_panel[0, 0]
    back = back_panel[0, 0]
    width = couple.shape[0]
    rows = probe_cells.shape[0]
    column, row, core = lax.axis_index("gx"), lax.axis_index("gy"), lax.axis_index("gz")
    x_bit, y_bit = column % 2, row % 2
    first_cell = ((column - x_bit) * lax.axis_size("gy") + row) * width
    place = jnp.stack([2 * y_bit + x_bit, core, first_cell, first_cell + lax.axis_size("gy") * width]).astype(jnp.int32)

    def split(kernel, size, value):
        return split_call(kernel, place, size, value, from_partner(value, "gz"))

    tall, wide, edge = (tall_kernel, 4 * width), (wide_kernel, 4 * width), (edge_kernel, 2 * width)

    couple_mine, lift_half = cut_call(place, (couple, lift), ((width // 2, 2 * width), (width, 2 * width)))
    back_half, root_half = cut_call(after(place, lift_half), (back, root), ((2 * width, width),) * 2)
    couple_other = from_partner(couple_mine, "gx")
    lift_y = from_partner(lift_half, "gy")
    lift_x = from_partner(lift_half, "gx")
    back_y = from_partner(back_half, "gy")
    lift_own = split_call(wide_kernel, place, wide[1], after(lift, root_half))
    root_own = split_call(tall_kernel, place, tall[1], after(root, root_half))
    back_own = split_call(tall_kernel, place, tall[1], after(back, root_half))
    edge_half = small_call(
        edge_state_kernel,
        (width + 3 * rows + 8, width),
        after(place, lift_own[0], root_own[0], back_own[0]),
        couple_mine,
        couple_other,
        pair_cols,
        probe_cells[None, :],
        adjoint_one_start[0, 0],
        adjoint_two_start[0, 0],
        mass_two[0],
    )
    root_x = from_partner(after(root_half, couple_other), "gx")
    edge_y = from_partner(after(edge_half, lift_y), "gy")
    edge_own = split(*edge, edge_half)
    back_x = from_partner(after(back_half, lift_x, edge_own[0]), "gx")
    lift_y_split = split(*wide, lift_y)
    root_y = from_partner(after(root_half, back_y, lift_y_split[0]), "gy")
    lift_x_split = split(*wide, lift_x)
    edge_x = from_partner(after(edge_half, root_x, lift_x_split[0]), "gx")
    back_y_split = split(*tall, back_y)
    lift_d = from_partner(after(lift_x, edge_y, back_y_split[0]), "gy")
    edge_y_split = split(*edge, edge_y)
    edge_d = from_partner(after(edge_y, back_x, edge_y_split[0]), "gx")
    root_x_split = split(*tall, root_x)
    root_d = from_partner(after(root_x, root_y, root_x_split[0]), "gy")
    root_y_split = split(*tall, root_y)
    back_d = from_partner(after(back_y, edge_x, root_y_split[0]), "gx")
    back_x_split = split(*tall, back_x)
    edge_x_split = split(*edge, edge_x)
    lift_d_split = split(*wide, lift_d)
    edge_d_split = split(*edge, edge_d)
    back_d = after(back_d, back_x_split[0], edge_x_split[0])
    root_d = after(root_d, lift_d_split[0], edge_d_split[0])

    vmem = pl.BlockSpec(memory_space=pltpu.VMEM)
    panels = edge_own + edge_x_split + edge_y_split + edge_d_split + lift_own + lift_x_split + lift_y_split + lift_d_split
    panels += root_own + root_x_split + root_y_split + back_own + back_x_split + back_y_split
    panels = tuple(pltpu.with_memory_space_constraint(panel, pltpu.VMEM) for panel in panels)
    panels += (root_d, from_partner(root_d, "gz"), back_d, from_partner(back_d, "gz"))
    one, two = pl.pallas_call(
        march_kernel,
        in_specs=[vmem] * 5 + [pl.BlockSpec(memory_space=pltpu.SMEM)] + [vmem] * len(panels),
        out_specs=(vmem, vmem),
        out_shape=(jax.ShapeDtypeStruct((rows, width), F32),) * 2,
        scratch_shapes=[pltpu.VMEM((4 * width, width), BF16)] * 4,
        compiler_params=pltpu.CompilerParams(vmem_limit_bytes=12 * 2**20),
    )(edge_half, edge_x, edge_y, edge_d, probe_weight, place, *panels)
    return (one[None, None], two[None, None])


def solution(mesh):
    placed = (
        P(("groups", "gx"), "gy", "gz", None),
        P(("groups", "gx"), "gy", "gz", None),
        P(("groups", "gx"), "gy", None, None),
        P(("groups", "gx"), "gy", None, None),
        P(("groups", "gx"), "gy", None, None),
        P(("groups", "gx"), "gy", None, None),
        P(("groups", "gx"), "gy", None, None),
        P(("groups", "gx"), "gy", None),
        P(("groups", "gz")),
        P("groups", "gz"),
    )
    return jax.shard_map(
        shards,
        mesh=mesh,
        in_specs=placed,
        out_specs=(P(("groups", "gx"), "gy", "gz", None), P(("groups", "gx"), "gy", "gz", None)),
        check_vma=False,
    )
```

```python
import jax
import jax.numpy as jnp
from jax import lax
from jax.experimental import pallas as pl
from jax.experimental.pallas import tpu as pltpu
from jax.sharding import PartitionSpec as P

F32 = jnp.float32
BF16 = jnp.bfloat16


def from_partner(value, axis):
    pairs = [(source, source ^ 1) for source in range(lax.axis_size(axis))]
    return lax.ppermute(value, axis, pairs)


def after(value, *earlier):
    return lax.optimization_barrier((value,) + earlier)[0]


def exact_dot(left, right):
    return jnp.dot(left, right, precision=lax.Precision.HIGHEST, preferred_element_type=F32)


def halves_of(value):
    high = value.astype(BF16)
    return high, (value - high.astype(F32)).astype(BF16)


def store_split(high_ref, low_ref, where, value):
    high, low = halves_of(value)
    high_ref[where] = high
    low_ref[where] = low


CHEAP = pl.CostEstimate(flops=1, transcendentals=0, bytes_accessed=1)


def cut_kernel(place, *refs):
    count = (len(refs) - 1) // 2
    panels, halves, sems = refs[:count], refs[count:2 * count], refs[-1]
    copies = []
    for index, (panel, half) in enumerate(zip(panels, halves)):
        rows, columns = half.shape
        if columns < panel.shape[1]:
            source = panel.at[:, pl.ds(pl.multiple_of(place[1] * columns, columns), columns)]
        else:
            source = panel.at[pl.ds(pl.multiple_of(place[1] * rows, rows), rows), :]
        copies.append(pltpu.make_async_copy(source, half, sems.at[index]))
    for copy in copies:
        copy.start()
    for copy in copies:
        copy.wait()


def cut_call(place, panels, shapes):
    hbm = [pltpu.with_memory_space_constraint(panel, pltpu.HBM) for panel in panels]
    return pl.pallas_call(
        cut_kernel,
        in_specs=[pl.BlockSpec(memory_space=pltpu.SMEM)] + [pl.BlockSpec(memory_space=pl.ANY)] * len(panels),
        out_specs=[pl.BlockSpec(memory_space=pl.ANY)] * len(panels),
        out_shape=[jax.ShapeDtypeStruct(shape, F32) for shape in shapes],
        scratch_shapes=[pltpu.SemaphoreType.DMA((len(panels),))],
        cost_estimate=CHEAP,
        compiler_params=pltpu.CompilerParams(vmem_limit_bytes=2**20),
    )(place, *hbm)


def column_of(row):
    shape = (row.shape[1], row.shape[1])
    same = lax.broadcasted_iota(jnp.int32, shape, 0) == lax.broadcasted_iota(jnp.int32, shape, 1)
    return jnp.sum(jnp.where(same, row, 0.0), axis=1, keepdims=True)


def edge_state_kernel(place, mine, other, pair_cols, cells, one, two, mass, edge_ref):
    half = mine.shape[0]
    rows, width = one.shape
    for step, couple in enumerate((mine, other)):
        start = ((place[0] % 2) ^ step) * half
        edge_ref[pl.ds(pl.multiple_of(start, half), half), :] = exact_dot(couple[...], pair_cols[...])
    cell = column_of(cells[...].astype(F32))
    number = lax.broadcasted_iota(jnp.int32, (rows, width), 1)
    chosen = [(cell == (number + place[2 + side]).astype(F32)).astype(F32) for side in range(2)]
    picked = exact_dot(jnp.concatenate(chosen, axis=1), pair_cols[...])
    for index, value in enumerate((one[...], two[...], picked)):
        edge_ref[2 * half + index * rows:2 * half + (index + 1) * rows, :] = value
    edge_ref[2 * half + 3 * rows:, :] = jnp.broadcast_to(mass[...], (8, width))


def small_call(kernel, shape, *values):
    vmem = pl.BlockSpec(memory_space=pltpu.VMEM)
    return pl.pallas_call(
        kernel,
        in_specs=[pl.BlockSpec(memory_space=pltpu.SMEM)] + [vmem] * (len(values) - 1),
        out_specs=vmem,
        out_shape=jax.ShapeDtypeStruct(shape, F32),
        cost_estimate=CHEAP,
        compiler_params=pltpu.CompilerParams(vmem_limit_bytes=6 * 2**20),
    )(*values)


def split_tall(place, pieces, high_ref, low_ref):
    width = high_ref.shape[1]
    blocks = 4 // len(pieces)
    for part, piece in enumerate(pieces):
        for block in range(blocks):
            number = block if len(pieces) == 1 else 2 * (place[1] ^ part) + block
            rows = pl.ds(pl.multiple_of((number ^ place[0]) * width, width), width)
            store_split(high_ref, low_ref, (rows, slice(None)), piece[block * width:(block + 1) * width, :])


def tall_kernel(place, *refs):
    split_tall(place, refs[:-2], *refs[-2:])


def wide_kernel(place, *refs):
    pieces, (high_ref, low_ref) = refs[:-2], refs[-2:]
    width = high_ref.shape[1]
    blocks = 4 // len(pieces)
    for part, piece in enumerate(pieces):
        for block in range(blocks):
            number = block if len(pieces) == 1 else 2 * (place[1] ^ part) + block
            rows = pl.ds(pl.multiple_of((number ^ place[0]) * width, width), width)
            store_split(high_ref, low_ref, (rows, slice(None)), piece[:, block * width:(block + 1) * width])


def edge_kernel(place, *refs):
    pieces, (high_ref, low_ref) = refs[:-2], refs[-2:]
    rows = pieces[0].shape[1] // 2
    for part, piece in enumerate(pieces):
        for bit in range(2):
            start = (bit ^ (place[0] % 2)) * 2 * rows + (place[1] ^ part) * rows
            where = (pl.ds(pl.multiple_of(start, rows), rows), slice(None))
            store_split(high_ref, low_ref, where, piece[bit * rows:(bit + 1) * rows, :])


def split_call(kernel, place, rows, *pieces):
    out = jax.ShapeDtypeStruct((rows, pieces[0].shape[1]), BF16)
    if kernel is wide_kernel:
        out = jax.ShapeDtypeStruct((rows, pieces[0].shape[0]), BF16)
    vmem = pl.BlockSpec(memory_space=pltpu.VMEM)
    return pl.pallas_call(
        kernel,
        in_specs=[pl.BlockSpec(memory_space=pltpu.SMEM)] + [vmem] * len(pieces),
        out_specs=(vmem, vmem),
        out_shape=(pltpu.VMEM(out.shape, BF16),) * 2,
        cost_estimate=CHEAP,
        compiler_params=pltpu.CompilerParams(vmem_limit_bytes=4 * 2**20),
    )(place, *pieces)


def product(left, high, low):
    rows = left.shape[0]
    left_high, left_low = halves_of(left)
    both = jnp.dot(jnp.concatenate([left_high, left_low], axis=0), high, preferred_element_type=F32)
    rest = jnp.dot(left_high, low, preferred_element_type=F32)
    return both[:rows] + both[rows:] + rest


def forward_half(one, picked, weights, edge):
    width = edge[0].shape[1]
    pairs = [one[:, side * 2 * width:(side + 1) * 2 * width] for side in range(2)]
    blocks = [product(pairs[tile // 2], edge[2 * tile][...], edge[2 * tile + 1][...]) for tile in range(4)]
    return jnp.concatenate(blocks, axis=1) + column_of(weights) * picked


def tall(left, panels):
    return jnp.concatenate([product(left, panels[2 * tile][...], panels[2 * tile + 1][...]) for tile in range(4)], axis=1)


def forward_two(half, two, scale, lift, root):
    width = lift[0].shape[1]

    def column_block(block, part):
        return jnp.concatenate([lift[2 * tile + part][block * width:(block + 1) * width, :] for tile in range(4)], axis=0)

    sums = jnp.concatenate([product(half, column_block(block, 0), column_block(block, 1)) for block in range(4)], axis=1)
    return tall(sums + two * scale, root)


def below(tiles, rows, index, count):
    start = tiles[0].shape[1] + index * rows
    return jnp.concatenate([tile[start:start + count, :] for tile in tiles], axis=1)


def march_kernel(s0, s1, s2, s3, weight, place, *refs):
    edge, lift, root, back = refs[:8], refs[8:16], refs[16:22], refs[22:28]
    root_mine, root_other, back_mine, back_other, one_ref, two_ref = refs[28:34]
    rows, width = one_ref.shape
    tiles = (s0, s1, s2, s3)
    split_tall(place, (root_mine, root_other), *refs[34:36])
    split_tall(place, (back_mine, back_other), *refs[36:38])
    root, back = root + refs[34:36], back + refs[36:38]
    one, two, picked, scale = [below(tiles, rows, index, count) for index, count in enumerate((rows, rows, rows, 1))]
    half = forward_half(one, picked, weight[0:1, :], edge)
    two = forward_two(half, two, scale, lift, root)

    def advance(step, carry):
        half, two = carry
        half = forward_half(half - tall(two, back), picked, weight[pl.ds(step, 1), :], edge)
        return half, forward_two(half, two, scale, lift, root)

    half, two = lax.fori_loop(1, weight.shape[0], advance, (half, two))
    one_ref[...] = half[:, :width] - product(two, back[0][...], back[1][...])
    two_ref[...] = two[:, :width]


def shards(
    adjoint_one_start,
    adjoint_two_start,
    couple_panel,
    pair_panel,
    lift_panel,
    root_panel,
    back_panel,
    mass_two,
    probe_cells,
    probe_weight,
):
    couple = couple_panel[0, 0]
    pair_cols = pair_panel[0, 0]
    lift = lift_panel[0, 0]
    root = root_panel[0, 0]
    back = back_panel[0, 0]
    width = couple.shape[0]
    rows = probe_cells.shape[0]
    column, row, core = lax.axis_index("gx"), lax.axis_index("gy"), lax.axis_index("gz")
    x_bit, y_bit = column % 2, row % 2
    first_cell = ((column - x_bit) * lax.axis_size("gy") + row) * width
    place = jnp.stack([2 * y_bit + x_bit, core, first_cell, first_cell + lax.axis_size("gy") * width]).astype(jnp.int32)

    tall, wide, edge = (tall_kernel, 4 * width), (wide_kernel, 4 * width), (edge_kernel, 2 * width)

    couple_mine, lift_half = cut_call(place, (couple, lift), ((width // 2, 2 * width), (width, 2 * width)))

    token = [place]
    waiting = []
    done = {}

    def arrive(name, value, kernel=None, size=0, ready=()):
        token[0] = after(value, token[0], *[done[other][0] for other in ready])
        if kernel is not None:
            waiting.append((name, kernel, size, token[0]))
        return token[0]

    def send(value, axis):
        return from_partner(after(value, token[0]), axis)

    def swap(count=1):
        for _ in range(count):
            name, kernel, size, value = waiting.pop(0)
            done[name] = (kernel, size, value, send(value, "gz"))

    def split(*names):
        for name in names:
            kernel, size, *pieces = done[name]
            done[name] = split_call(kernel, after(place, token[0]), size, *pieces)

    couple_other = from_partner(couple_mine, "gx")
    lift_y = from_partner(lift_half, "gy")
    lift_x = from_partner(lift_half, "gx")
    back_half, root_half = cut_call(after(place, couple_other), (back, root), ((2 * width, width),) * 2)
    done["L"] = split_call(wide_kernel, place, wide[1], after(lift, lift_half))
    done["R"] = split_call(tall_kernel, place, tall[1], after(root, lift_half))
    done["B"] = split_call(tall_kernel, place, tall[1], after(back, lift_half))
    couple_other = arrive("C", couple_other)
    root_x = send(root_half, "gx")
    back_y = send(back_half, "gy")
    edge_half = small_call(
        edge_state_kernel,
        (width + 3 * rows + 8, width),
        place,
        couple_mine,
        couple_other,
        pair_cols,
        probe_cells[None, :],
        adjoint_one_start[0, 0],
        adjoint_two_start[0, 0],
        mass_two[0],
    )
    waiting.append(("E", *edge, edge_half))
    lift_y = arrive("Ly", lift_y, *wide)
    edge_y = send(edge_half, "gy")
    lift_x = arrive("Lx", lift_x, *wide)
    back_x = send(back_half, "gx")
    swap()
    back_y = arrive("By", back_y, *tall, ready=("L",))
    root_y = send(root_half, "gy")
    swap()
    root_x = arrive("Rx", root_x, *tall, ready=("R",))
    edge_x = send(edge_half, "gx")
    swap()
    split("E")
    edge_y = arrive("Ey", edge_y, *edge, ready=("B",))
    lift_d = send(lift_x, "gy")
    swap()
    split("Ly")
    back_x = arrive("Bx", back_x, *tall, ready=("E",))
    edge_d = send(edge_y, "gx")
    swap()
    split("Lx")
    root_y = arrive("Ry", root_y, *tall, ready=("Ly",))
    root_d = send(root_x, "gy")
    swap()
    split("By")
    edge_x = arrive("Ex", edge_x, *edge, ready=("Lx",))
    back_d = send(back_y, "gx")
    swap()
    split("Rx")
    lift_d = arrive("Ld", lift_d, *wide, ready=("By",))
    swap()
    split("Ey")
    edge_d = arrive("Ed", edge_d, *edge, ready=("Rx", "Ey"))
    swap()
    split("Bx", "Ry")
    root_d = arrive("Rd", root_d, ready=("Bx", "Ry"))
    swap(2)
    split("Ex")
    back_d = arrive("Bd", back_d, ready=("Ex",))
    split("Ld", "Ed")

    vmem, smem = pl.BlockSpec(memory_space=pltpu.VMEM), pl.BlockSpec(memory_space=pltpu.SMEM)
    panels = done["E"] + done["Ex"] + done["Ey"] + done["Ed"] + done["L"] + done["Lx"] + done["Ly"] + done["Ld"]
    panels += done["R"] + done["Rx"] + done["Ry"] + done["B"] + done["Bx"] + done["By"]
    panels += (root_d, from_partner(root_d, "gz"), back_d, from_partner(back_d, "gz"))
    one, two = pl.pallas_call(
        march_kernel,
        in_specs=[vmem] * 5 + [smem] + [vmem] * len(panels),
        out_specs=(vmem, vmem),
        out_shape=(jax.ShapeDtypeStruct((rows, width), F32),) * 2,
        scratch_shapes=[pltpu.VMEM((4 * width, width), BF16)] * 4,
        compiler_params=pltpu.CompilerParams(vmem_limit_bytes=12 * 2**20),
    )(edge_half, edge_x, edge_y, edge_d, probe_weight, place, *panels)
    return (one[None, None], two[None, None])


def solution(mesh):
    placed = (
        P(("groups", "gx"), "gy", "gz", None),
        P(("groups", "gx"), "gy", "gz", None),
        P(("groups", "gx"), "gy", None, None),
        P(("groups", "gx"), "gy", None, None),
        P(("groups", "gx"), "gy", None, None),
        P(("groups", "gx"), "gy", None, None),
        P(("groups", "gx"), "gy", None, None),
        P(("groups", "gx"), "gy", None),
        P(("groups", "gz")),
        P("groups", "gz"),
    )
    return jax.shard_map(
        shards,
        mesh=mesh,
        in_specs=placed,
        out_specs=(P(("groups", "gx"), "gy", "gz", None), P(("groups", "gx"), "gy", "gz", None)),
        check_vma=False,
    )
```

```python
import jax
import jax.numpy as jnp
from jax import lax
from jax.experimental import pallas as pl
from jax.experimental.pallas import tpu as pltpu
from jax.sharding import PartitionSpec as P

F32 = jnp.float32
BF16 = jnp.bfloat16


def from_partner(value, axis):
    pairs = [(source, source ^ 1) for source in range(lax.axis_size(axis))]
    return lax.ppermute(value, axis, pairs)


def after(value, *earlier):
    return lax.optimization_barrier((value,) + earlier)[0]


def exact_dot(left, right):
    return jnp.dot(left, right, precision=lax.Precision.HIGHEST, preferred_element_type=F32)


def halves_of(value):
    high = value.astype(BF16)
    return high, (value - high.astype(F32)).astype(BF16)


def store_split(high_ref, low_ref, where, value):
    high, low = halves_of(value)
    high_ref[where] = high
    low_ref[where] = low


PLAN = (
    ("take", "Cx"), ("send", "Rx"), ("send", "By"), ("edge", "E"),
    ("take", "Ly"), ("send", "Ey"),
    ("take", "Lx", "B"), ("send", "Bx"), ("swap", "E"),
    ("take", "By", "L"), ("send", "Ry"), ("swap", "Ly"),
    ("take", "Rx", "R"), ("send", "Ex"), ("swap", "Lx"), ("split", "E"),
    ("take", "Ey"), ("send", "Ld"), ("swap", "By"), ("split", "Ly"),
    ("take", "Bx", "E"), ("send", "Ed"), ("swap", "Rx"), ("split", "Lx"),
    ("take", "Ry", "Ly"), ("send", "Rd"), ("swap", "Ey"),
    ("take", "Ex", "Lx"), ("send", "Bd"), ("swap", "Bx"), ("split", "By"), ("split", "Rx"),
    ("take", "Ld"), ("swap", "Ry"), ("swap", "Ld"), ("split", "Ey"),
    ("take", "Ed", "By", "Rx", "Ey"), ("swap", "Ex"), ("swap", "Ed"), ("split", "Bx"), ("split", "Ry"), ("split", "Ld"),
    ("take", "Rd", "Ld"), ("swap", "Rd"), ("split", "Ex"), ("split", "Ed"),
    ("take", "Bd", "Ex", "Ed"), ("swap", "Bd"),
)


CHEAP = pl.CostEstimate(flops=1, transcendentals=0, bytes_accessed=1)


def cut_kernel(place, *refs):
    count = (len(refs) - 1) // 2
    panels, halves, sems = refs[:count], refs[count:2 * count], refs[-1]
    copies = []
    for index, (panel, half) in enumerate(zip(panels, halves)):
        rows, columns = half.shape
        if columns < panel.shape[1]:
            source = panel.at[:, pl.ds(pl.multiple_of(place[1] * columns, columns), columns)]
        else:
            source = panel.at[pl.ds(pl.multiple_of(place[1] * rows, rows), rows), :]
        copies.append(pltpu.make_async_copy(source, half, sems.at[index]))
    for copy in copies:
        copy.start()
    for copy in copies:
        copy.wait()


def cut_call(place, panels, shapes):
    hbm = [pltpu.with_memory_space_constraint(panel, pltpu.HBM) for panel in panels]
    return pl.pallas_call(
        cut_kernel,
        in_specs=[pl.BlockSpec(memory_space=pltpu.SMEM)] + [pl.BlockSpec(memory_space=pl.ANY)] * len(panels),
        out_specs=[pl.BlockSpec(memory_space=pl.ANY)] * len(panels),
        out_shape=[jax.ShapeDtypeStruct(shape, F32) for shape in shapes],
        scratch_shapes=[pltpu.SemaphoreType.DMA((len(panels),))],
        cost_estimate=CHEAP,
        compiler_params=pltpu.CompilerParams(vmem_limit_bytes=2**20),
    )(place, *hbm)


def column_of(row):
    shape = (row.shape[1], row.shape[1])
    same = lax.broadcasted_iota(jnp.int32, shape, 0) == lax.broadcasted_iota(jnp.int32, shape, 1)
    return jnp.sum(jnp.where(same, row, 0.0), axis=1, keepdims=True)


def edge_state_kernel(place, mine, other, pair_cols, cells, one, two, mass, weight, edge_ref, weight_ref):
    half = mine.shape[0]
    rows, width = one.shape
    for step, couple in enumerate((mine, other)):
        start = ((place[0] % 2) ^ step) * half
        edge_ref[pl.ds(pl.multiple_of(start, half), half), :] = exact_dot(couple[...], pair_cols[...])
    cell = column_of(cells[...].astype(F32))
    number = lax.broadcasted_iota(jnp.int32, (rows, width), 1)
    chosen = [(cell == (number + place[2 + side]).astype(F32)).astype(F32) for side in range(2)]
    picked = exact_dot(jnp.concatenate(chosen, axis=1), pair_cols[...])
    for index, value in enumerate((one[...], two[...], picked)):
        edge_ref[2 * half + index * rows:2 * half + (index + 1) * rows, :] = value
    edge_ref[2 * half + 3 * rows:, :] = jnp.broadcast_to(mass[...], (8, width))
    weight_ref[...] = weight[...]


def edge_call(rows, place, *values):
    vmem = pl.BlockSpec(memory_space=pltpu.VMEM)
    shapes = ((rows, values[2].shape[1]), values[-1].shape)
    return pl.pallas_call(
        edge_state_kernel,
        in_specs=[pl.BlockSpec(memory_space=pltpu.SMEM)] + [vmem] * len(values),
        out_specs=(vmem, vmem),
        out_shape=tuple(jax.ShapeDtypeStruct(shape, F32) for shape in shapes),
        cost_estimate=CHEAP,
        compiler_params=pltpu.CompilerParams(vmem_limit_bytes=6 * 2**20),
    )(place, *values)


def split_tall(place, pieces, high_ref, low_ref):
    width = high_ref.shape[1]
    blocks = 4 // len(pieces)
    for part, piece in enumerate(pieces):
        for block in range(blocks):
            number = block if len(pieces) == 1 else 2 * (place[1] ^ part) + block
            rows = pl.ds(pl.multiple_of((number ^ place[0]) * width, width), width)
            store_split(high_ref, low_ref, (rows, slice(None)), piece[block * width:(block + 1) * width, :])


def tall_kernel(place, *refs):
    split_tall(place, refs[:-2], *refs[-2:])


def wide_kernel(place, *refs):
    pieces, (high_ref, low_ref) = refs[:-2], refs[-2:]
    width = high_ref.shape[1]
    blocks = 4 // len(pieces)
    for part, piece in enumerate(pieces):
        for block in range(blocks):
            number = block if len(pieces) == 1 else 2 * (place[1] ^ part) + block
            rows = pl.ds(pl.multiple_of((number ^ place[0]) * width, width), width)
            store_split(high_ref, low_ref, (rows, slice(None)), piece[:, block * width:(block + 1) * width])


def edge_kernel(place, *refs):
    pieces, (high_ref, low_ref) = refs[:-2], refs[-2:]
    rows = pieces[0].shape[1] // 2
    for part, piece in enumerate(pieces):
        for bit in range(2):
            start = (bit ^ (place[0] % 2)) * 2 * rows + (place[1] ^ part) * rows
            where = (pl.ds(pl.multiple_of(start, rows), rows), slice(None))
            store_split(high_ref, low_ref, where, piece[bit * rows:(bit + 1) * rows, :])


def split_call(kernel, place, rows, *pieces):
    out = jax.ShapeDtypeStruct((rows, pieces[0].shape[1]), BF16)
    if kernel is wide_kernel:
        out = jax.ShapeDtypeStruct((rows, pieces[0].shape[0]), BF16)
    vmem = pl.BlockSpec(memory_space=pltpu.VMEM)
    return pl.pallas_call(
        kernel,
        in_specs=[pl.BlockSpec(memory_space=pltpu.SMEM)] + [vmem] * len(pieces),
        out_specs=(vmem, vmem),
        out_shape=(pltpu.VMEM(out.shape, BF16),) * 2,
        cost_estimate=CHEAP,
        compiler_params=pltpu.CompilerParams(vmem_limit_bytes=4 * 2**20),
    )(place, *pieces)


def product(left, high, low):
    rows = left.shape[0]
    left_high, left_low = halves_of(left)
    both = jnp.dot(jnp.concatenate([left_high, left_low], axis=0), high, preferred_element_type=F32)
    rest = jnp.dot(left_high, low, preferred_element_type=F32)
    return both[:rows] + both[rows:] + rest


def forward_half(one, picked, weights, edge):
    width = edge[0].shape[1]
    pairs = [one[:, side * 2 * width:(side + 1) * 2 * width] for side in range(2)]
    blocks = [product(pairs[tile // 2], edge[2 * tile][...], edge[2 * tile + 1][...]) for tile in range(4)]
    return jnp.concatenate(blocks, axis=1) + column_of(weights) * picked


def tall(left, panels):
    return jnp.concatenate([product(left, panels[2 * tile][...], panels[2 * tile + 1][...]) for tile in range(4)], axis=1)


def forward_two(half, two, scale, lift, root):
    width = lift[0].shape[1]

    def column_block(block, part):
        return jnp.concatenate([lift[2 * tile + part][block * width:(block + 1) * width, :] for tile in range(4)], axis=0)

    sums = jnp.concatenate([product(half, column_block(block, 0), column_block(block, 1)) for block in range(4)], axis=1)
    return tall(sums + two * scale, root)


def below(tiles, rows, index, count):
    start = tiles[0].shape[1] + index * rows
    return jnp.concatenate([tile[start:start + count, :] for tile in tiles], axis=1)


def march_kernel(s0, s1, s2, s3, weight, place, *refs):
    edge, lift, root, back = refs[:8], refs[8:16], refs[16:22], refs[22:28]
    root_mine, root_other, back_mine, back_other, one_ref, two_ref = refs[28:34]
    rows, width = one_ref.shape
    tiles = (s0, s1, s2, s3)
    split_tall(place, (root_mine, root_other), *refs[34:36])
    split_tall(place, (back_mine, back_other), *refs[36:38])
    root, back = root + refs[34:36], back + refs[36:38]
    one, two, picked, scale = [below(tiles, rows, index, count) for index, count in enumerate((rows, rows, rows, 1))]
    half = forward_half(one, picked, weight[0:1, :], edge)
    two = forward_two(half, two, scale, lift, root)

    def advance(step, carry):
        half, two = carry
        half = forward_half(half - tall(two, back), picked, weight[pl.ds(step, 1), :], edge)
        return half, forward_two(half, two, scale, lift, root)

    half, two = lax.fori_loop(1, weight.shape[0], advance, (half, two))
    one_ref[...] = half[:, :width] - product(two, back[0][...], back[1][...])
    two_ref[...] = two[:, :width]


def shards(
    adjoint_one_start,
    adjoint_two_start,
    couple_panel,
    pair_panel,
    lift_panel,
    root_panel,
    back_panel,
    mass_two,
    probe_cells,
    probe_weight,
):
    couple = couple_panel[0, 0]
    pair_cols = pair_panel[0, 0]
    lift = lift_panel[0, 0]
    root = root_panel[0, 0]
    back = back_panel[0, 0]
    width = couple.shape[0]
    rows = probe_cells.shape[0]
    column, row, core = lax.axis_index("gx"), lax.axis_index("gy"), lax.axis_index("gz")
    x_bit, y_bit = column % 2, row % 2
    first_cell = ((column - x_bit) * lax.axis_size("gy") + row) * width
    place = jnp.stack([2 * y_bit + x_bit, core, first_cell, first_cell + lax.axis_size("gy") * width]).astype(jnp.int32)

    couple_half, lift_half = cut_call(place, (couple, lift), ((width // 2, 2 * width), (width, 2 * width)))
    value = {"Cx": from_partner(couple_half, "gx"), "Ly": from_partner(lift_half, "gy"), "Lx": from_partner(lift_half, "gx")}
    back_half, root_half = cut_call(after(place, value["Cx"]), (back, root), ((2 * width, width),) * 2)
    own = {"L": lift_half, "B": back_half, "R": root_half}
    kernels = {"L": (wide_kernel, 4 * width), "R": (tall_kernel, 4 * width), "B": (tall_kernel, 4 * width), "E": (edge_kernel, 2 * width)}
    whole = after(place, lift_half)
    ready = {
        name: split_call(kernels[name][0], whole, kernels[name][1], panel)
        for name, panel in (("L", lift), ("R", root), ("B", back))
    }
    other = {}
    token = place
    for verb, name, *earlier in PLAN:
        kind, where = name[0], name[1:]
        if verb == "take":
            token = value[name] = after(value[name], token, *[ready[panel][0] for panel in earlier])
        elif verb == "edge":
            own["E"], weight = edge_call(
                width + 3 * rows + 8,
                place,
                couple_half,
                value["Cx"],
                pair_cols,
                probe_cells[None, :],
                adjoint_one_start[0, 0],
                adjoint_two_start[0, 0],
                mass_two[0],
                probe_weight,
            )
            value["E"] = own["E"]
        elif verb == "send":
            axis = where if where != "d" else "x" if kind in "EB" else "y"
            source = own[kind] if where != "d" else value[kind + ("y" if axis == "x" else "x")]
            value[name] = from_partner(after(source, token), "g" + axis)
        elif verb == "swap":
            other[name] = from_partner(after(value[name], token), "gz")
        else:
            kernel, size = kernels[kind]
            ready[name] = split_call(kernel, after(place, token), size, value[name], other[name])

    vmem, smem = pl.BlockSpec(memory_space=pltpu.VMEM), pl.BlockSpec(memory_space=pltpu.SMEM)
    panels = ()
    for kind, tiles in (("E", ("", "x", "y", "d")), ("L", ("", "x", "y", "d")), ("R", ("", "x", "y")), ("B", ("", "x", "y"))):
        for tile in tiles:
            panels += ready[kind + tile]
    panels += (value["Rd"], other["Rd"], value["Bd"], other["Bd"])
    one, two = pl.pallas_call(
        march_kernel,
        in_specs=[vmem] * 5 + [smem] + [vmem] * len(panels),
        out_specs=(vmem, vmem),
        out_shape=(jax.ShapeDtypeStruct((rows, width), F32),) * 2,
        scratch_shapes=[pltpu.VMEM((4 * width, width), BF16)] * 4,
        compiler_params=pltpu.CompilerParams(vmem_limit_bytes=12 * 2**20),
    )(own["E"], value["Ex"], value["Ey"], value["Ed"], weight, place, *panels)
    return (one[None, None], two[None, None])


def solution(mesh):
    placed = (
        P(("groups", "gx"), "gy", "gz", None),
        P(("groups", "gx"), "gy", "gz", None),
        P(("groups", "gx"), "gy", None, None),
        P(("groups", "gx"), "gy", None, None),
        P(("groups", "gx"), "gy", None, None),
        P(("groups", "gx"), "gy", None, None),
        P(("groups", "gx"), "gy", None, None),
        P(("groups", "gx"), "gy", None),
        P(("groups", "gz")),
        P("groups", "gz"),
    )
    return jax.shard_map(
        shards,
        mesh=mesh,
        in_specs=placed,
        out_specs=(P(("groups", "gx"), "gy", "gz", None), P(("groups", "gx"), "gy", "gz", None)),
        check_vma=False,
    )
```

```python
import jax
import jax.numpy as jnp
from jax import lax
from jax.experimental import pallas as pl
from jax.experimental.pallas import tpu as pltpu
from jax.sharding import PartitionSpec as P

F32 = jnp.float32
BF16 = jnp.bfloat16


def from_partner(value, axis):
    pairs = [(source, source ^ 1) for source in range(lax.axis_size(axis))]
    return lax.ppermute(value, axis, pairs)


def after(value, *earlier):
    return lax.optimization_barrier((value,) + earlier)[0]


def exact_dot(left, right):
    return jnp.dot(left, right, precision=lax.Precision.HIGHEST, preferred_element_type=F32)


def halves_of(value):
    high = value.astype(BF16)
    return high, (value - high.astype(F32)).astype(BF16)


def store_split(high_ref, low_ref, where, value):
    high, low = halves_of(value)
    high_ref[where] = high
    low_ref[where] = low


PLAN = (
    ("take", "Cx"), ("send", "Rx"), ("send", "By"), ("edge", "E"),
    ("take", "Ly"), ("send", "Ey"),
    ("take", "Lx"), ("send", "Bx"), ("swap", "E"),
    ("take", "By", "L"), ("send", "Ry"), ("swap", "Ly"),
    ("take", "Rx", "R", "B"), ("send", "Ex"), ("swap", "Lx"), ("split", "E"),
    ("take", "Ey"), ("send", "Ld"), ("split", "Ly"),
    ("take", "Bx", "E"), ("send", "Ed"), ("swap", "By"), ("swap", "Rx"), ("split", "Rx"),
    ("take", "Ry", "Ly"), ("send", "Rd"), ("swap", "Ey"), ("swap", "Bx"), ("split", "Lx"),
    ("take", "Ex", "Rx"), ("send", "Bd"),
    ("take", "Ld", "Lx"), ("swap", "Ry"), ("swap", "Ld"), ("split", "By"), ("split", "Ey"), ("split", "Bx"),
    ("take", "Ed", "Ey"), ("swap", "Ex"), ("swap", "Ed"), ("split", "Ry"), ("split", "Ex"), ("split", "Ld"),
    ("take", "Rd", "By"), ("swap", "Rd"), ("split", "Ed"),
    ("take", "Bd", "Ex", "Ld", "Ed"), ("swap", "Bd"),
)


CHEAP = pl.CostEstimate(flops=1, transcendentals=0, bytes_accessed=1)


def cut_kernel(place, *refs):
    count = (len(refs) - 1) // 2
    panels, halves, sems = refs[:count], refs[count:2 * count], refs[-1]
    copies = []
    for index, (panel, half) in enumerate(zip(panels, halves)):
        rows, columns = half.shape
        if columns < panel.shape[1]:
            source = panel.at[:, pl.ds(pl.multiple_of(place[1] * columns, columns), columns)]
        else:
            source = panel.at[pl.ds(pl.multiple_of(place[1] * rows, rows), rows), :]
        copies.append(pltpu.make_async_copy(source, half, sems.at[index]))
    for copy in copies:
        copy.start()
    for copy in copies:
        copy.wait()


def cut_call(place, panels, shapes):
    hbm = [pltpu.with_memory_space_constraint(panel, pltpu.HBM) for panel in panels]
    return pl.pallas_call(
        cut_kernel,
        in_specs=[pl.BlockSpec(memory_space=pltpu.SMEM)] + [pl.BlockSpec(memory_space=pl.ANY)] * len(panels),
        out_specs=[pl.BlockSpec(memory_space=pl.ANY)] * len(panels),
        out_shape=[jax.ShapeDtypeStruct(shape, F32) for shape in shapes],
        scratch_shapes=[pltpu.SemaphoreType.DMA((len(panels),))],
        cost_estimate=CHEAP,
        compiler_params=pltpu.CompilerParams(vmem_limit_bytes=2**20),
    )(place, *hbm)


def column_of(row):
    shape = (row.shape[1], row.shape[1])
    same = lax.broadcasted_iota(jnp.int32, shape, 0) == lax.broadcasted_iota(jnp.int32, shape, 1)
    return jnp.sum(jnp.where(same, row, 0.0), axis=1, keepdims=True)


def edge_state_kernel(place, mine, other, pair_cols, cells, one, two, mass, weight, edge_ref, weight_ref):
    half = mine.shape[0]
    rows, width = one.shape
    for step, couple in enumerate((mine, other)):
        start = ((place[0] % 2) ^ step) * half
        edge_ref[pl.ds(pl.multiple_of(start, half), half), :] = exact_dot(couple[...], pair_cols[...])
    cell = column_of(cells[...].astype(F32))
    number = lax.broadcasted_iota(jnp.int32, (rows, width), 1)
    chosen = [(cell == (number + place[2 + side]).astype(F32)).astype(F32) for side in range(2)]
    picked = exact_dot(jnp.concatenate(chosen, axis=1), pair_cols[...])
    for index, value in enumerate((one[...], two[...], picked)):
        edge_ref[2 * half + index * rows:2 * half + (index + 1) * rows, :] = value
    edge_ref[2 * half + 3 * rows:, :] = jnp.broadcast_to(mass[...], (8, width))
    weight_ref[...] = weight[...]


def edge_call(rows, place, *values):
    vmem = pl.BlockSpec(memory_space=pltpu.VMEM)
    shapes = ((rows, values[2].shape[1]), values[-1].shape)
    return pl.pallas_call(
        edge_state_kernel,
        in_specs=[pl.BlockSpec(memory_space=pltpu.SMEM)] + [vmem] * len(values),
        out_specs=(vmem, vmem),
        out_shape=tuple(jax.ShapeDtypeStruct(shape, F32) for shape in shapes),
        cost_estimate=CHEAP,
        compiler_params=pltpu.CompilerParams(vmem_limit_bytes=6 * 2**20),
    )(place, *values)


def split_tall(place, pieces, high_ref, low_ref):
    width = high_ref.shape[1]
    blocks = 4 // len(pieces)
    for part, piece in enumerate(pieces):
        for block in range(blocks):
            number = block if len(pieces) == 1 else 2 * (place[1] ^ part) + block
            rows = pl.ds(pl.multiple_of((number ^ place[0]) * width, width), width)
            store_split(high_ref, low_ref, (rows, slice(None)), piece[block * width:(block + 1) * width, :])


def tall_kernel(place, *refs):
    split_tall(place, refs[:-2], *refs[-2:])


def wide_kernel(place, *refs):
    pieces, (high_ref, low_ref) = refs[:-2], refs[-2:]
    width = high_ref.shape[1]
    blocks = 4 // len(pieces)
    for part, piece in enumerate(pieces):
        for block in range(blocks):
            number = block if len(pieces) == 1 else 2 * (place[1] ^ part) + block
            rows = pl.ds(pl.multiple_of((number ^ place[0]) * width, width), width)
            store_split(high_ref, low_ref, (rows, slice(None)), piece[:, block * width:(block + 1) * width])


def edge_kernel(place, *refs):
    pieces, (high_ref, low_ref) = refs[:-2], refs[-2:]
    rows = pieces[0].shape[1] // 2
    for part, piece in enumerate(pieces):
        for bit in range(2):
            start = (bit ^ (place[0] % 2)) * 2 * rows + (place[1] ^ part) * rows
            where = (pl.ds(pl.multiple_of(start, rows), rows), slice(None))
            store_split(high_ref, low_ref, where, piece[bit * rows:(bit + 1) * rows, :])


def split_call(kernel, place, rows, *pieces):
    out = jax.ShapeDtypeStruct((rows, pieces[0].shape[1]), BF16)
    if kernel is wide_kernel:
        out = jax.ShapeDtypeStruct((rows, pieces[0].shape[0]), BF16)
    vmem = pl.BlockSpec(memory_space=pltpu.VMEM)
    return pl.pallas_call(
        kernel,
        in_specs=[pl.BlockSpec(memory_space=pltpu.SMEM)] + [vmem] * len(pieces),
        out_specs=(vmem, vmem),
        out_shape=(pltpu.VMEM(out.shape, BF16),) * 2,
        cost_estimate=CHEAP,
        compiler_params=pltpu.CompilerParams(vmem_limit_bytes=4 * 2**20),
    )(place, *pieces)


def product(left, high, low):
    rows = left.shape[0]
    left_high, left_low = halves_of(left)
    both = jnp.dot(jnp.concatenate([left_high, left_low], axis=0), high, preferred_element_type=F32)
    rest = jnp.dot(left_high, low, preferred_element_type=F32)
    return both[:rows] + both[rows:] + rest


def forward_half(one, picked, weights, edge):
    width = edge[0].shape[1]
    pairs = [one[:, side * 2 * width:(side + 1) * 2 * width] for side in range(2)]
    blocks = [product(pairs[tile // 2], edge[2 * tile][...], edge[2 * tile + 1][...]) for tile in range(4)]
    return jnp.concatenate(blocks, axis=1) + column_of(weights) * picked


def tall(left, panels):
    return jnp.concatenate([product(left, panels[2 * tile][...], panels[2 * tile + 1][...]) for tile in range(4)], axis=1)


def forward_two(half, two, scale, lift, root):
    width = lift[0].shape[1]

    def column_block(block, part):
        return jnp.concatenate([lift[2 * tile + part][block * width:(block + 1) * width, :] for tile in range(4)], axis=0)

    sums = jnp.concatenate([product(half, column_block(block, 0), column_block(block, 1)) for block in range(4)], axis=1)
    return tall(sums + two * scale, root)


def below(tiles, rows, index, count):
    start = tiles[0].shape[1] + index * rows
    return jnp.concatenate([tile[start:start + count, :] for tile in tiles], axis=1)


def march_kernel(s0, s1, s2, s3, weight, place, *refs):
    edge, lift, root, back = refs[:8], refs[8:16], refs[16:22], refs[22:28]
    root_mine, root_other, back_mine, back_other, one_ref, two_ref = refs[28:34]
    rows, width = one_ref.shape
    tiles = (s0, s1, s2, s3)
    split_tall(place, (root_mine, root_other), *refs[34:36])
    split_tall(place, (back_mine, back_other), *refs[36:38])
    root, back = root + refs[34:36], back + refs[36:38]
    one, two, picked, scale = [below(tiles, rows, index, count) for index, count in enumerate((rows, rows, rows, 1))]
    half = forward_half(one, picked, weight[0:1, :], edge)
    two = forward_two(half, two, scale, lift, root)

    def advance(step, carry):
        half, two = carry
        half = forward_half(half - tall(two, back), picked, weight[pl.ds(step, 1), :], edge)
        return half, forward_two(half, two, scale, lift, root)

    half, two = lax.fori_loop(1, weight.shape[0], advance, (half, two))
    one_ref[...] = half[:, :width] - product(two, back[0][...], back[1][...])
    two_ref[...] = two[:, :width]


def shards(
    adjoint_one_start,
    adjoint_two_start,
    couple_panel,
    pair_panel,
    lift_panel,
    root_panel,
    back_panel,
    mass_two,
    probe_cells,
    probe_weight,
):
    couple = couple_panel[0, 0]
    pair_cols = pair_panel[0, 0]
    lift = lift_panel[0, 0]
    root = root_panel[0, 0]
    back = back_panel[0, 0]
    width = couple.shape[0]
    rows = probe_cells.shape[0]
    column, row, core = lax.axis_index("gx"), lax.axis_index("gy"), lax.axis_index("gz")
    x_bit, y_bit = column % 2, row % 2
    first_cell = ((column - x_bit) * lax.axis_size("gy") + row) * width
    place = jnp.stack([2 * y_bit + x_bit, core, first_cell, first_cell + lax.axis_size("gy") * width]).astype(jnp.int32)

    couple_half, lift_half = cut_call(place, (couple, lift), ((width // 2, 2 * width), (width, 2 * width)))
    value = {"Cx": from_partner(couple_half, "gx"), "Ly": from_partner(lift_half, "gy"), "Lx": from_partner(lift_half, "gx")}
    back_half, root_half = cut_call(after(place, value["Cx"]), (back, root), ((2 * width, width),) * 2)
    own = {"L": lift_half, "B": back_half, "R": root_half}
    kernels = {"L": (wide_kernel, 4 * width), "R": (tall_kernel, 4 * width), "B": (tall_kernel, 4 * width), "E": (edge_kernel, 2 * width)}
    whole = after(place, lift_half)
    ready = {
        name: split_call(kernels[name][0], whole, kernels[name][1], panel)
        for name, panel in (("L", lift), ("R", root), ("B", back))
    }
    other = {}
    token = place
    for verb, name, *earlier in PLAN:
        kind, where = name[0], name[1:]
        if verb == "take":
            token = value[name] = after(value[name], token, *[ready[panel][0] for panel in earlier])
        elif verb == "edge":
            own["E"], weight = edge_call(
                width + 3 * rows + 8,
                place,
                couple_half,
                value["Cx"],
                pair_cols,
                probe_cells[None, :],
                adjoint_one_start[0, 0],
                adjoint_two_start[0, 0],
                mass_two[0],
                probe_weight,
            )
            value["E"] = own["E"]
        elif verb == "send":
            axis = where if where != "d" else "x" if kind in "EB" else "y"
            source = own[kind] if where != "d" else value[kind + ("y" if axis == "x" else "x")]
            value[name] = from_partner(after(source, token), "g" + axis)
        elif verb == "swap":
            other[name] = from_partner(after(value[name], token), "gz")
        else:
            kernel, size = kernels[kind]
            ready[name] = split_call(kernel, after(place, token), size, value[name], other[name])

    vmem, smem = pl.BlockSpec(memory_space=pltpu.VMEM), pl.BlockSpec(memory_space=pltpu.SMEM)
    panels = ()
    for kind, tiles in (("E", ("", "x", "y", "d")), ("L", ("", "x", "y", "d")), ("R", ("", "x", "y")), ("B", ("", "x", "y"))):
        for tile in tiles:
            panels += ready[kind + tile]
    panels += (value["Rd"], other["Rd"], value["Bd"], other["Bd"])
    one, two = pl.pallas_call(
        march_kernel,
        in_specs=[vmem] * 5 + [smem] + [vmem] * len(panels),
        out_specs=(vmem, vmem),
        out_shape=(jax.ShapeDtypeStruct((rows, width), F32),) * 2,
        scratch_shapes=[pltpu.VMEM((4 * width, width), BF16)] * 4,
        compiler_params=pltpu.CompilerParams(vmem_limit_bytes=12 * 2**20),
    )(own["E"], value["Ex"], value["Ey"], value["Ed"], weight, place, *panels)
    return (one[None, None], two[None, None])


def solution(mesh):
    placed = (
        P(("groups", "gx"), "gy", "gz", None),
        P(("groups", "gx"), "gy", "gz", None),
        P(("groups", "gx"), "gy", None, None),
        P(("groups", "gx"), "gy", None, None),
        P(("groups", "gx"), "gy", None, None),
        P(("groups", "gx"), "gy", None, None),
        P(("groups", "gx"), "gy", None, None),
        P(("groups", "gx"), "gy", None),
        P(("groups", "gz")),
        P("groups", "gz"),
    )
    return jax.shard_map(
        shards,
        mesh=mesh,
        in_specs=placed,
        out_specs=(P(("groups", "gx"), "gy", "gz", None), P(("groups", "gx"), "gy", "gz", None)),
        check_vma=False,
    )
```

```python
import jax
import jax.numpy as jnp
from jax import lax
from jax.experimental import pallas as pl
from jax.experimental.pallas import tpu as pltpu
from jax.sharding import PartitionSpec as P

F32 = jnp.float32
BF16 = jnp.bfloat16


def from_partner(value, axis):
    pairs = [(source, source ^ 1) for source in range(lax.axis_size(axis))]
    return lax.ppermute(value, axis, pairs)


def couple_across(couple):
    columns, cores = lax.axis_size("gx"), lax.axis_size("gz")
    pairs = [(column * cores + column % 2, (column ^ 1) * cores + column % 2) for column in range(columns)]
    return lax.ppermute(couple, ("gx", "gz"), pairs)


def after(value, *earlier):
    return lax.optimization_barrier((value,) + earlier)[0]


def exact_dot(left, right):
    return jnp.dot(left, right, precision=lax.Precision.HIGHEST, preferred_element_type=F32)


def halves_of(value):
    high = value.astype(BF16)
    return high, (value - high.astype(F32)).astype(BF16)


def store_split(high_ref, low_ref, where, value):
    high, low = halves_of(value)
    high_ref[where] = high
    low_ref[where] = low


PLAN = (
    ("take", "Cx"), ("send", "Rx"), ("send", "By"), ("edge", "E"),
    ("take", "Ly"), ("send", "Bx"), ("send", "Ey"),
    ("take", "Lx"), ("swap", "E"),
    ("take", "By", "L"), ("send", "Ry"), ("swap", "Ly"),
    ("take", "Rx", "R", "B"), ("send", "Ex"), ("swap", "Lx"), ("split", "E"),
    ("take", "Ey", "E"), ("send", "Ld"), ("split", "Ly"),
    ("take", "Bx", "Ly"), ("send", "Ed"), ("swap", "By"), ("swap", "Rx"), ("split", "Rx"),
    ("take", "Ry"), ("send", "Rd"), ("swap", "Ey"), ("swap", "Bx"), ("split", "Lx"),
    ("take", "Ex", "Rx"), ("send", "Bd"),
    ("take", "Ld", "Lx"), ("swap", "Ry"), ("swap", "Ex"), ("swap", "Ld"), ("split", "By"), ("split", "Ey"), ("split", "Bx"), ("split", "Ex"),
    ("take", "Ed", "Ey"), ("swap", "Ed"), ("split", "Ry"), ("split", "Ld"),
    ("take", "Rd", "By", "Ex"), ("swap", "Rd"), ("split", "Ed"), ("lead", "lead"),
    ("take", "Bd", "Ld", "Ed", "lead"), ("swap", "Bd"),
)


CHEAP = pl.CostEstimate(flops=1, transcendentals=0, bytes_accessed=1)


def cut_kernel(place, *refs):
    count = (len(refs) - 1) // 2
    panels, halves, sems = refs[:count], refs[count:2 * count], refs[-1]
    copies = []
    for index, (panel, half) in enumerate(zip(panels, halves)):
        rows, columns = half.shape
        if columns < panel.shape[1]:
            source = panel.at[:, pl.ds(pl.multiple_of(place[1] * columns, columns), columns)]
        else:
            source = panel.at[pl.ds(pl.multiple_of(place[1] * rows, rows), rows), :]
        copies.append(pltpu.make_async_copy(source, half, sems.at[index]))
    for copy in copies:
        copy.start()
    for copy in copies:
        copy.wait()


def cut_call(place, panels, shapes):
    hbm = [pltpu.with_memory_space_constraint(panel, pltpu.HBM) for panel in panels]
    return pl.pallas_call(
        cut_kernel,
        in_specs=[pl.BlockSpec(memory_space=pltpu.SMEM)] + [pl.BlockSpec(memory_space=pl.ANY)] * len(panels),
        out_specs=[pl.BlockSpec(memory_space=pl.ANY)] * len(panels),
        out_shape=[jax.ShapeDtypeStruct(shape, F32) for shape in shapes],
        scratch_shapes=[pltpu.SemaphoreType.DMA((len(panels),))],
        cost_estimate=CHEAP,
        compiler_params=pltpu.CompilerParams(vmem_limit_bytes=2**20),
    )(place, *hbm)


def column_of(row):
    shape = (row.shape[1], row.shape[1])
    same = lax.broadcasted_iota(jnp.int32, shape, 0) == lax.broadcasted_iota(jnp.int32, shape, 1)
    return jnp.sum(jnp.where(same, row, 0.0), axis=1, keepdims=True)


def edge_state_kernel(place, mine, other, pair_cols, cells, one, two, mass, weight, edge_ref, weight_ref):
    rows, width = one.shape
    couple = jnp.where(place[0] % 2 == place[1], mine[...], other[...])
    edge_ref[:width, :] = exact_dot(couple, pair_cols[...])
    cell = column_of(cells[...].astype(F32))
    number = lax.broadcasted_iota(jnp.int32, (rows, width), 1)
    chosen = [(cell == (number + place[2 + side]).astype(F32)).astype(F32) for side in range(2)]
    picked = exact_dot(jnp.concatenate(chosen, axis=1), pair_cols[...])
    for index, value in enumerate((one[...], two[...], picked)):
        edge_ref[width + index * rows:width + (index + 1) * rows, :] = value
    edge_ref[width + 3 * rows:, :] = jnp.broadcast_to(mass[...], (8, width))
    weight_ref[...] = weight[...]


def edge_call(rows, place, *values):
    vmem = pl.BlockSpec(memory_space=pltpu.VMEM)
    shapes = ((rows, values[2].shape[1]), values[-1].shape)
    return pl.pallas_call(
        edge_state_kernel,
        in_specs=[pl.BlockSpec(memory_space=pltpu.SMEM)] + [vmem] * len(values),
        out_specs=(vmem, vmem),
        out_shape=tuple(jax.ShapeDtypeStruct(shape, F32) for shape in shapes),
        cost_estimate=CHEAP,
        compiler_params=pltpu.CompilerParams(vmem_limit_bytes=6 * 2**20),
    )(place, *values)


def split_tall(place, pieces, high_ref, low_ref):
    width = high_ref.shape[1]
    blocks = 4 // len(pieces)
    for part, piece in enumerate(pieces):
        for block in range(blocks):
            number = block if len(pieces) == 1 else 2 * (place[1] ^ part) + block
            rows = pl.ds(pl.multiple_of((number ^ place[0]) * width, width), width)
            store_split(high_ref, low_ref, (rows, slice(None)), piece[block * width:(block + 1) * width, :])


def tall_kernel(place, *refs):
    split_tall(place, refs[:-2], *refs[-2:])


def wide_kernel(place, *refs):
    pieces, (high_ref, low_ref) = refs[:-2], refs[-2:]
    width = high_ref.shape[1]
    blocks = 4 // len(pieces)
    for part, piece in enumerate(pieces):
        for block in range(blocks):
            number = block if len(pieces) == 1 else 2 * (place[1] ^ part) + block
            rows = pl.ds(pl.multiple_of((number ^ place[0]) * width, width), width)
            store_split(high_ref, low_ref, (rows, slice(None)), piece[:, block * width:(block + 1) * width])


def edge_kernel(place, *refs):
    pieces, (high_ref, low_ref) = refs[:-2], refs[-2:]
    width = high_ref.shape[1]
    for part, piece in enumerate(pieces):
        start = (place[1] ^ part ^ (place[0] % 2)) * width
        store_split(high_ref, low_ref, (pl.ds(pl.multiple_of(start, width), width), slice(None)), piece[:width, :])


def split_call(kernel, place, rows, *pieces):
    out = jax.ShapeDtypeStruct((rows, pieces[0].shape[1]), BF16)
    if kernel is wide_kernel:
        out = jax.ShapeDtypeStruct((rows, pieces[0].shape[0]), BF16)
    vmem = pl.BlockSpec(memory_space=pltpu.VMEM)
    return pl.pallas_call(
        kernel,
        in_specs=[pl.BlockSpec(memory_space=pltpu.SMEM)] + [vmem] * len(pieces),
        out_specs=(vmem, vmem),
        out_shape=(pltpu.VMEM(out.shape, BF16),) * 2,
        cost_estimate=CHEAP,
        compiler_params=pltpu.CompilerParams(vmem_limit_bytes=4 * 2**20),
    )(place, *pieces)


def product(left, high, low):
    rows = left.shape[0]
    left_high, left_low = halves_of(left)
    both = jnp.dot(jnp.concatenate([left_high, left_low], axis=0), high, preferred_element_type=F32)
    rest = jnp.dot(left_high, low, preferred_element_type=F32)
    return both[:rows] + both[rows:] + rest


def forward_half(one, picked, weights, edge):
    width = edge[0].shape[1]
    pairs = [one[:, side * 2 * width:(side + 1) * 2 * width] for side in range(2)]
    blocks = [product(pairs[tile // 2], edge[2 * tile][...], edge[2 * tile + 1][...]) for tile in range(4)]
    return jnp.concatenate(blocks, axis=1) + column_of(weights) * picked


def tall(left, panels):
    return jnp.concatenate([product(left, panels[2 * tile][...], panels[2 * tile + 1][...]) for tile in range(4)], axis=1)


def quad_sums(half, two, scale, lift):
    width = lift[0].shape[1]

    def column_block(block, part):
        return jnp.concatenate([lift[2 * tile + part][block * width:(block + 1) * width, :] for tile in range(4)], axis=0)

    sums = jnp.concatenate([product(half, column_block(block, 0), column_block(block, 1)) for block in range(4)], axis=1)
    return sums + two * scale


def below(tiles, rows, index, count):
    start = tiles[0].shape[1] + index * rows
    return jnp.concatenate([tile[start:start + count, :] for tile in tiles], axis=1)


def lead_kernel(s0, s1, s2, s3, weight, *refs):
    edge, lift, (half_ref, sums_ref) = refs[:8], refs[8:16], refs[16:]
    tiles, rows = (s0, s1, s2, s3), half_ref.shape[0]
    one, two, picked, scale = [below(tiles, rows, index, count) for index, count in enumerate((rows, rows, rows, 1))]
    half_ref[...] = forward_half(one, picked, weight[0:1, :], edge)
    sums_ref[...] = quad_sums(half_ref[...], two, scale, lift)


def march_kernel(s0, s1, s2, s3, weight, half_start, sums_start, place, *refs):
    edge, lift, root, back = refs[:8], refs[8:16], refs[16:22], refs[22:28]
    root_mine, root_other, back_mine, back_other, one_ref, two_ref = refs[28:34]
    rows, width = one_ref.shape
    tiles = (s0, s1, s2, s3)
    split_tall(place, (root_mine, root_other), *refs[34:36])
    split_tall(place, (back_mine, back_other), *refs[36:38])
    root, back = root + refs[34:36], back + refs[36:38]
    picked, scale = below(tiles, rows, 2, rows), below(tiles, rows, 3, 1)

    def advance(step, carry):
        half, two = carry
        half = forward_half(half - tall(two, back), picked, weight[pl.ds(step, 1), :], edge)
        return half, tall(quad_sums(half, two, scale, lift), root)

    half, two = lax.fori_loop(1, weight.shape[0], advance, (half_start[...], tall(sums_start[...], root)))
    one_ref[...] = half[:, :width] - product(two, back[0][...], back[1][...])
    two_ref[...] = two[:, :width]


def shards(
    adjoint_one_start,
    adjoint_two_start,
    couple_panel,
    pair_panel,
    lift_panel,
    root_panel,
    back_panel,
    mass_two,
    probe_cells,
    probe_weight,
):
    couple = couple_panel[0, 0]
    pair_cols = pair_panel[0, 0]
    lift = lift_panel[0, 0]
    root = root_panel[0, 0]
    back = back_panel[0, 0]
    width = couple.shape[0]
    rows = probe_cells.shape[0]
    column, row, core = lax.axis_index("gx"), lax.axis_index("gy"), lax.axis_index("gz")
    x_bit, y_bit = column % 2, row % 2
    first_cell = ((column - x_bit) * lax.axis_size("gy") + row) * width
    place = jnp.stack([2 * y_bit + x_bit, core, first_cell, first_cell + lax.axis_size("gy") * width]).astype(jnp.int32)

    (lift_half,) = cut_call(place, (lift,), ((width, 2 * width),))
    value = {"Cx": couple_across(couple), "Ly": from_partner(lift_half, "gy"), "Lx": from_partner(lift_half, "gx")}
    back_half, root_half = cut_call(after(place, value["Cx"]), (back, root), ((2 * width, width),) * 2)
    own = {"L": lift_half, "B": back_half, "R": root_half}
    kernels = {"L": (wide_kernel, 4 * width), "R": (tall_kernel, 4 * width), "B": (tall_kernel, 4 * width), "E": (edge_kernel, 2 * width)}
    whole = after(place, lift_half)
    ready = {
        name: split_call(kernels[name][0], whole, kernels[name][1], panel)
        for name, panel in (("L", lift), ("R", root), ("B", back))
    }
    other = {}
    token = place
    for verb, name, *earlier in PLAN:
        kind, where = name[0], name[1:]
        if verb == "take":
            token = value[name] = after(value[name], token, *[ready[panel][0] for panel in earlier])
        elif verb == "edge":
            own["E"], weight = edge_call(
                width + 3 * rows + 8,
                place,
                couple,
                value["Cx"],
                pair_cols,
                probe_cells[None, :],
                adjoint_one_start[0, 0],
                adjoint_two_start[0, 0],
                mass_two[0],
                probe_weight,
            )
            value["E"] = own["E"]
        elif verb == "send":
            axis = where if where != "d" else "x" if kind in "EB" else "y"
            source = own[kind] if where != "d" else value[kind + ("y" if axis == "x" else "x")]
            value[name] = from_partner(after(source, token), "g" + axis)
        elif verb == "swap":
            other[name] = from_partner(after(value[name], token), "gz")
        elif verb == "lead":
            states = (own["E"], value["Ex"], value["Ey"], value["Ed"], weight)
            early = [panel for tile in ("E", "Ex", "Ey", "Ed", "L", "Lx", "Ly", "Ld") for panel in ready[tile]]
            ready[name] = pl.pallas_call(
                lead_kernel,
                in_specs=[pl.BlockSpec(memory_space=pltpu.VMEM)] * (5 + len(early)),
                out_specs=(pl.BlockSpec(memory_space=pltpu.VMEM),) * 2,
                out_shape=(jax.ShapeDtypeStruct((rows, 4 * width), F32),) * 2,
                cost_estimate=CHEAP,
                compiler_params=pltpu.CompilerParams(vmem_limit_bytes=6 * 2**20),
            )(*states, *early)
        else:
            kernel, size = kernels[kind]
            ready[name] = split_call(kernel, after(place, token), size, value[name], other[name])

    vmem, smem = pl.BlockSpec(memory_space=pltpu.VMEM), pl.BlockSpec(memory_space=pltpu.SMEM)
    late = [panel for tile in ("R", "Rx", "Ry", "B", "Bx", "By") for panel in ready[tile]]
    late += [value["Rd"], other["Rd"], value["Bd"], other["Bd"]]
    one, two = pl.pallas_call(
        march_kernel,
        in_specs=[vmem] * 7 + [smem] + [vmem] * (len(early) + len(late)),
        out_specs=(vmem, vmem),
        out_shape=(jax.ShapeDtypeStruct((rows, width), F32),) * 2,
        scratch_shapes=[pltpu.VMEM((4 * width, width), BF16)] * 4,
        compiler_params=pltpu.CompilerParams(vmem_limit_bytes=12 * 2**20),
    )(*states, *ready["lead"], place, *early, *late)
    return (one[None, None], two[None, None])


def solution(mesh):
    placed = (
        P(("groups", "gx"), "gy", "gz", None),
        P(("groups", "gx"), "gy", "gz", None),
        P(("groups", "gx"), "gy", None, None),
        P(("groups", "gx"), "gy", None, None),
        P(("groups", "gx"), "gy", None, None),
        P(("groups", "gx"), "gy", None, None),
        P(("groups", "gx"), "gy", None, None),
        P(("groups", "gx"), "gy", None),
        P(("groups", "gz")),
        P("groups", "gz"),
    )
    return jax.shard_map(
        shards,
        mesh=mesh,
        in_specs=placed,
        out_specs=(P(("groups", "gx"), "gy", "gz", None), P(("groups", "gx"), "gy", "gz", None)),
        check_vma=False,
    )
```

```python
import jax
import jax.numpy as jnp
from jax import lax
from jax.experimental import pallas as pl
from jax.experimental.pallas import tpu as pltpu
from jax.sharding import PartitionSpec as P

F32 = jnp.float32
BF16 = jnp.bfloat16


def from_partner(value, axis):
    pairs = [(source, source ^ 1) for source in range(lax.axis_size(axis))]
    return lax.ppermute(value, axis, pairs)


def after(value, *earlier):
    return lax.optimization_barrier((value,) + earlier)[0]


def exact_dot(left, right):
    return jnp.dot(left, right, precision=lax.Precision.HIGHEST, preferred_element_type=F32)


def halves_of(value):
    high = value.astype(BF16)
    return high, (value - high.astype(F32)).astype(BF16)


def store_split(high_ref, low_ref, where, value):
    high, low = halves_of(value)
    high_ref[where] = high
    low_ref[where] = low


PLAN = (
    ("take", "Cx"), ("send", "Rx"), ("send", "By"), ("edge", "E"),
    ("take", "Ly"), ("send", "Bx"), ("send", "Ey"),
    ("take", "Lx"), ("swap", "E"),
    ("take", "By", "L"), ("send", "Ry"), ("swap", "Ly"),
    ("take", "Rx", "R", "B"), ("send", "Ex"), ("swap", "Lx"), ("split", "E"),
    ("take", "Ey", "E"), ("send", "Ld"), ("split", "Ly"),
    ("take", "Bx", "Ly"), ("send", "Ed"), ("swap", "By"), ("swap", "Rx"), ("split", "By"), ("split", "Rx"),
    ("take", "Ry"), ("send", "Rd"), ("swap", "Ey"), ("split", "Lx"),
    ("take", "Ex", "Rx"), ("send", "Bd"),
    ("take", "Ld", "Lx"), ("swap", "Bx"), ("swap", "Ry"), ("swap", "Ex"), ("swap", "Ld"), ("split", "Ey"), ("split", "Ex"),
    ("take", "Ed", "By", "Ey"), ("swap", "Ed"), ("split", "Ld"),
    ("take", "Rd", "Ex"), ("swap", "Rd"), ("split", "Rd"), ("split", "Bx"), ("split", "Ed"), ("lead", "lead"),
    ("take", "Bd", "Ld", "Ed", "lead"), ("swap", "Bd"), ("split", "Ry"), ("root", "root"),
)


CHEAP = pl.CostEstimate(flops=1, transcendentals=0, bytes_accessed=1)


def cut_kernel(place, *refs):
    count = (len(refs) - 1) // 2
    panels, halves, sems = refs[:count], refs[count:2 * count], refs[-1]
    copies = []
    for index, (panel, half) in enumerate(zip(panels, halves)):
        rows, columns = half.shape
        if columns < panel.shape[1]:
            source = panel.at[:, pl.ds(pl.multiple_of(place[1] * columns, columns), columns)]
        else:
            source = panel.at[pl.ds(pl.multiple_of(place[1] * rows, rows), rows), :]
        copies.append(pltpu.make_async_copy(source, half, sems.at[index]))
    for copy in copies:
        copy.start()
    for copy in copies:
        copy.wait()


def cut_call(place, panels, shapes):
    hbm = [pltpu.with_memory_space_constraint(panel, pltpu.HBM) for panel in panels]
    return pl.pallas_call(
        cut_kernel,
        in_specs=[pl.BlockSpec(memory_space=pltpu.SMEM)] + [pl.BlockSpec(memory_space=pl.ANY)] * len(panels),
        out_specs=[pl.BlockSpec(memory_space=pl.ANY)] * len(panels),
        out_shape=[jax.ShapeDtypeStruct(shape, F32) for shape in shapes],
        scratch_shapes=[pltpu.SemaphoreType.DMA((len(panels),))],
        cost_estimate=CHEAP,
        compiler_params=pltpu.CompilerParams(vmem_limit_bytes=2**20),
    )(place, *hbm)


def column_of(row):
    shape = (row.shape[1], row.shape[1])
    same = lax.broadcasted_iota(jnp.int32, shape, 0) == lax.broadcasted_iota(jnp.int32, shape, 1)
    return jnp.sum(jnp.where(same, row, 0.0), axis=1, keepdims=True)


def edge_state_kernel(place, mine, other, pair_cols, cells, one, two, mass, weight, edge_ref, weight_ref):
    half = mine.shape[0]
    rows, width = one.shape
    for step, couple in enumerate((mine, other)):
        start = ((place[0] % 2) ^ step) * half
        edge_ref[pl.ds(pl.multiple_of(start, half), half), :] = exact_dot(couple[...], pair_cols[...])
    cell = column_of(cells[...].astype(F32))
    number = lax.broadcasted_iota(jnp.int32, (rows, width), 1)
    chosen = [(cell == (number + place[2 + side]).astype(F32)).astype(F32) for side in range(2)]
    picked = exact_dot(jnp.concatenate(chosen, axis=1), pair_cols[...])
    for index, value in enumerate((one[...], two[...], picked)):
        edge_ref[2 * half + index * rows:2 * half + (index + 1) * rows, :] = value
    edge_ref[2 * half + 3 * rows:, :] = jnp.broadcast_to(mass[...], (8, width))
    weight_ref[...] = weight[...]


def edge_call(rows, place, *values):
    vmem = pl.BlockSpec(memory_space=pltpu.VMEM)
    shapes = ((rows, values[2].shape[1]), values[-1].shape)
    return pl.pallas_call(
        edge_state_kernel,
        in_specs=[pl.BlockSpec(memory_space=pltpu.SMEM)] + [vmem] * len(values),
        out_specs=(vmem, vmem),
        out_shape=tuple(jax.ShapeDtypeStruct(shape, F32) for shape in shapes),
        cost_estimate=CHEAP,
        compiler_params=pltpu.CompilerParams(vmem_limit_bytes=6 * 2**20),
    )(place, *values)


def split_tall(place, pieces, high_ref, low_ref):
    width = high_ref.shape[1]
    blocks = 4 // len(pieces)
    for part, piece in enumerate(pieces):
        for block in range(blocks):
            number = block if len(pieces) == 1 else 2 * (place[1] ^ part) + block
            rows = pl.ds(pl.multiple_of((number ^ place[0]) * width, width), width)
            store_split(high_ref, low_ref, (rows, slice(None)), piece[block * width:(block + 1) * width, :])


def tall_kernel(place, *refs):
    split_tall(place, refs[:-2], *refs[-2:])


def wide_kernel(place, *refs):
    pieces, (high_ref, low_ref) = refs[:-2], refs[-2:]
    width = high_ref.shape[1]
    blocks = 4 // len(pieces)
    for part, piece in enumerate(pieces):
        for block in range(blocks):
            number = block if len(pieces) == 1 else 2 * (place[1] ^ part) + block
            rows = pl.ds(pl.multiple_of((number ^ place[0]) * width, width), width)
            store_split(high_ref, low_ref, (rows, slice(None)), piece[:, block * width:(block + 1) * width])


def edge_kernel(place, *refs):
    pieces, (high_ref, low_ref) = refs[:-2], refs[-2:]
    rows = pieces[0].shape[1] // 2
    for part, piece in enumerate(pieces):
        for bit in range(2):
            start = (bit ^ (place[0] % 2)) * 2 * rows + (place[1] ^ part) * rows
            where = (pl.ds(pl.multiple_of(start, rows), rows), slice(None))
            store_split(high_ref, low_ref, where, piece[bit * rows:(bit + 1) * rows, :])


def split_call(kernel, place, rows, *pieces):
    out = jax.ShapeDtypeStruct((rows, pieces[0].shape[1]), BF16)
    if kernel is wide_kernel:
        out = jax.ShapeDtypeStruct((rows, pieces[0].shape[0]), BF16)
    vmem = pl.BlockSpec(memory_space=pltpu.VMEM)
    return pl.pallas_call(
        kernel,
        in_specs=[pl.BlockSpec(memory_space=pltpu.SMEM)] + [vmem] * len(pieces),
        out_specs=(vmem, vmem),
        out_shape=(pltpu.VMEM(out.shape, BF16),) * 2,
        cost_estimate=CHEAP,
        compiler_params=pltpu.CompilerParams(vmem_limit_bytes=4 * 2**20),
    )(place, *pieces)


def product(left, high, low):
    rows = left.shape[0]
    left_high, left_low = halves_of(left)
    both = jnp.dot(jnp.concatenate([left_high, left_low], axis=0), high, preferred_element_type=F32)
    rest = jnp.dot(left_high, low, preferred_element_type=F32)
    return both[:rows] + both[rows:] + rest


def forward_half(one, picked, weights, edge):
    width = edge[0].shape[1]
    pairs = [one[:, side * 2 * width:(side + 1) * 2 * width] for side in range(2)]
    blocks = [product(pairs[tile // 2], edge[2 * tile][...], edge[2 * tile + 1][...]) for tile in range(4)]
    return jnp.concatenate(blocks, axis=1) + column_of(weights) * picked


def tall(left, panels):
    return jnp.concatenate([product(left, panels[2 * tile][...], panels[2 * tile + 1][...]) for tile in range(4)], axis=1)


def quad_sums(half, two, scale, lift):
    width = lift[0].shape[1]

    def column_block(block, part):
        return jnp.concatenate([lift[2 * tile + part][block * width:(block + 1) * width, :] for tile in range(4)], axis=0)

    sums = jnp.concatenate([product(half, column_block(block, 0), column_block(block, 1)) for block in range(4)], axis=1)
    return sums + two * scale


def below(tiles, rows, index, count):
    start = tiles[0].shape[1] + index * rows
    return jnp.concatenate([tile[start:start + count, :] for tile in tiles], axis=1)


def lead_kernel(s0, s1, s2, s3, weight, *refs):
    edge, lift, (half_ref, sums_ref) = refs[:8], refs[8:16], refs[16:]
    tiles, rows = (s0, s1, s2, s3), half_ref.shape[0]
    one, two, picked, scale = [below(tiles, rows, index, count) for index, count in enumerate((rows, rows, rows, 1))]
    half_ref[...] = forward_half(one, picked, weight[0:1, :], edge)
    sums_ref[...] = quad_sums(half_ref[...], two, scale, lift)


def root_kernel(sums, *refs):
    refs[-1][...] = tall(sums[...], refs[:-1])


def march_kernel(s0, s1, s2, s3, weight, half_start, two_start, place, *refs):
    edge, lift, root, back = refs[:8], refs[8:16], refs[16:24], refs[24:30]
    mine, other, one_ref, two_ref, last_high, last_low = refs[30:]
    rows, width = one_ref.shape
    tiles = (s0, s1, s2, s3)
    split_tall(place, (mine, other), last_high, last_low)
    back = back + (last_high, last_low)
    picked, scale = below(tiles, rows, 2, rows), below(tiles, rows, 3, 1)

    def advance(step, carry):
        half, two = carry
        half = forward_half(half - tall(two, back), picked, weight[pl.ds(step, 1), :], edge)
        return half, tall(quad_sums(half, two, scale, lift), root)

    half, two = lax.fori_loop(1, weight.shape[0], advance, (half_start[...], two_start[...]))
    one_ref[...] = half[:, :width] - product(two, back[0][...], back[1][...])
    two_ref[...] = two[:, :width]


def shards(
    adjoint_one_start,
    adjoint_two_start,
    couple_panel,
    pair_panel,
    lift_panel,
    root_panel,
    back_panel,
    mass_two,
    probe_cells,
    probe_weight,
):
    couple = couple_panel[0, 0]
    pair_cols = pair_panel[0, 0]
    lift = lift_panel[0, 0]
    root = root_panel[0, 0]
    back = back_panel[0, 0]
    width = couple.shape[0]
    rows = probe_cells.shape[0]
    column, row, core = lax.axis_index("gx"), lax.axis_index("gy"), lax.axis_index("gz")
    x_bit, y_bit = column % 2, row % 2
    first_cell = ((column - x_bit) * lax.axis_size("gy") + row) * width
    place = jnp.stack([2 * y_bit + x_bit, core, first_cell, first_cell + lax.axis_size("gy") * width]).astype(jnp.int32)

    couple_half, lift_half = cut_call(place, (couple, lift), ((width // 2, 2 * width), (width, 2 * width)))
    value = {"Cx": from_partner(couple_half, "gx"), "Ly": from_partner(lift_half, "gy"), "Lx": from_partner(lift_half, "gx")}
    back_half, root_half = cut_call(after(place, value["Cx"]), (back, root), ((2 * width, width),) * 2)
    own = {"L": lift_half, "B": back_half, "R": root_half}
    kernels = {"L": (wide_kernel, 4 * width), "R": (tall_kernel, 4 * width), "B": (tall_kernel, 4 * width), "E": (edge_kernel, 2 * width)}
    whole = after(place, lift_half)
    ready = {
        name: split_call(kernels[name][0], whole, kernels[name][1], panel)
        for name, panel in (("L", lift), ("R", root), ("B", back))
    }
    other = {}
    token = place
    for verb, name, *earlier in PLAN:
        kind, where = name[0], name[1:]
        if verb == "take":
            token = value[name] = after(value[name], token, *[ready[panel][0] for panel in earlier])
        elif verb == "edge":
            own["E"], weight = edge_call(
                width + 3 * rows + 8,
                place,
                couple_half,
                value["Cx"],
                pair_cols,
                probe_cells[None, :],
                adjoint_one_start[0, 0],
                adjoint_two_start[0, 0],
                mass_two[0],
                probe_weight,
            )
            value["E"] = own["E"]
        elif verb == "send":
            axis = where if where != "d" else "x" if kind in "EB" else "y"
            source = own[kind] if where != "d" else value[kind + ("y" if axis == "x" else "x")]
            value[name] = from_partner(after(source, token), "g" + axis)
        elif verb == "swap":
            other[name] = from_partner(after(value[name], token), "gz")
        elif verb == "lead":
            states = (own["E"], value["Ex"], value["Ey"], value["Ed"], weight)
            early = [panel for tile in ("E", "Ex", "Ey", "Ed", "L", "Lx", "Ly", "Ld") for panel in ready[tile]]
            ready[name] = pl.pallas_call(
                lead_kernel,
                in_specs=[pl.BlockSpec(memory_space=pltpu.VMEM)] * (5 + len(early)),
                out_specs=(pl.BlockSpec(memory_space=pltpu.VMEM),) * 2,
                out_shape=(jax.ShapeDtypeStruct((rows, 4 * width), F32),) * 2,
                cost_estimate=CHEAP,
                compiler_params=pltpu.CompilerParams(vmem_limit_bytes=6 * 2**20),
            )(*states, *early)
        elif verb == "root":
            roots = [panel for tile in ("R", "Rx", "Ry", "Rd") for panel in ready[tile]]
            two = pl.pallas_call(
                root_kernel,
                in_specs=[pl.BlockSpec(memory_space=pltpu.VMEM)] * (1 + len(roots)),
                out_specs=pl.BlockSpec(memory_space=pltpu.VMEM),
                out_shape=jax.ShapeDtypeStruct((rows, 4 * width), F32),
                cost_estimate=CHEAP,
                compiler_params=pltpu.CompilerParams(vmem_limit_bytes=6 * 2**20),
            )(ready["lead"][1], *roots)
        else:
            kernel, size = kernels[kind]
            ready[name] = split_call(kernel, after(place, token), size, value[name], other[name])

    vmem, smem = pl.BlockSpec(memory_space=pltpu.VMEM), pl.BlockSpec(memory_space=pltpu.SMEM)
    late = [panel for tile in ("B", "Bx", "By") for panel in ready[tile]] + [value["Bd"], other["Bd"]]
    one, two = pl.pallas_call(
        march_kernel,
        in_specs=[vmem] * 7 + [smem] + [vmem] * (len(early) + len(roots) + len(late)),
        out_specs=(vmem, vmem),
        out_shape=(jax.ShapeDtypeStruct((rows, width), F32),) * 2,
        scratch_shapes=[pltpu.VMEM((4 * width, width), BF16)] * 2,
        compiler_params=pltpu.CompilerParams(vmem_limit_bytes=12 * 2**20),
    )(*states, ready["lead"][0], two, place, *early, *roots, *late)
    return (one[None, None], two[None, None])


def solution(mesh):
    placed = (
        P(("groups", "gx"), "gy", "gz", None),
        P(("groups", "gx"), "gy", "gz", None),
        P(("groups", "gx"), "gy", None, None),
        P(("groups", "gx"), "gy", None, None),
        P(("groups", "gx"), "gy", None, None),
        P(("groups", "gx"), "gy", None, None),
        P(("groups", "gx"), "gy", None, None),
        P(("groups", "gx"), "gy", None),
        P(("groups", "gz")),
        P("groups", "gz"),
    )
    return jax.shard_map(
        shards,
        mesh=mesh,
        in_specs=placed,
        out_specs=(P(("groups", "gx"), "gy", "gz", None), P(("groups", "gx"), "gy", "gz", None)),
        check_vma=False,
    )
```

```python
import jax
import jax.numpy as jnp
from jax import lax
from jax.experimental import pallas as pl
from jax.experimental.pallas import tpu as pltpu
from jax.sharding import PartitionSpec as P

F32 = jnp.float32
BF16 = jnp.bfloat16


def from_partner(value, axis):
    pairs = [(source, source ^ 1) for source in range(lax.axis_size(axis))]
    return lax.ppermute(value, axis, pairs)


def after(value, *earlier):
    return lax.optimization_barrier((value,) + earlier)[0]


def exact_dot(left, right):
    return jnp.dot(left, right, precision=lax.Precision.HIGHEST, preferred_element_type=F32)


def halves_of(value):
    high = value.astype(BF16)
    return high, (value - high.astype(F32)).astype(BF16)


def store_split(high_ref, low_ref, start, piece, row, column, size):
    step = 32
    for offset in range(0, size, step):
        value = piece[row + offset:row + offset + step, column:column + high_ref.shape[1]]
        where = pl.ds(pl.multiple_of(start + offset, step), step)
        high_ref[where, :], low_ref[where, :] = halves_of(value)


PLAN = (
    ("take", "Cx"), ("send", "Rx"), ("send", "By"), ("edge", "E"),
    ("take", "Ly"), ("send", "Bx"), ("send", "Ey"),
    ("take", "Lx"), ("swap", "E"),
    ("take", "By", "L"), ("send", "Ry"), ("swap", "Ly"),
    ("take", "Rx", "R", "B"), ("send", "Ex"), ("swap", "Lx"), ("split", "E"),
    ("take", "Ey", "E"), ("send", "Ld"), ("split", "Ly"),
    ("take", "Bx", "Ly"), ("send", "Ed"), ("swap", "By"), ("swap", "Rx"), ("split", "By"), ("split", "Rx"),
    ("take", "Ry"), ("send", "Rd"), ("swap", "Ey"), ("split", "Lx"),
    ("take", "Ex", "Rx"), ("send", "Bd"),
    ("take", "Ld", "Lx"), ("swap", "Bx"), ("swap", "Ry"), ("swap", "Ex"), ("swap", "Ld"), ("split", "Ey"), ("split", "Ex"),
    ("take", "Ed", "By", "Ey"), ("swap", "Ed"), ("split", "Ld"),
    ("take", "Rd", "Ex"), ("swap", "Rd"), ("split", "Rd"), ("split", "Bx"), ("split", "Ed"), ("lead", "lead"),
    ("take", "Bd", "Ld", "Ed", "lead"), ("swap", "Bd"), ("split", "Ry"), ("root", "root"),
)


CHEAP = pl.CostEstimate(flops=1, transcendentals=0, bytes_accessed=1)


def cut_kernel(place, *refs):
    count = (len(refs) - 1) // 2
    panels, halves, sems = refs[:count], refs[count:2 * count], refs[-1]
    copies = []
    for index, (panel, half) in enumerate(zip(panels, halves)):
        rows, columns = half.shape
        if columns < panel.shape[1]:
            source = panel.at[:, pl.ds(pl.multiple_of(place[1] * columns, columns), columns)]
        else:
            source = panel.at[pl.ds(pl.multiple_of(place[1] * rows, rows), rows), :]
        copies.append(pltpu.make_async_copy(source, half, sems.at[index]))
    for copy in copies:
        copy.start()
    for copy in copies:
        copy.wait()


def cut_call(place, panels, shapes):
    hbm = [pltpu.with_memory_space_constraint(panel, pltpu.HBM) for panel in panels]
    return pl.pallas_call(
        cut_kernel,
        in_specs=[pl.BlockSpec(memory_space=pltpu.SMEM)] + [pl.BlockSpec(memory_space=pl.ANY)] * len(panels),
        out_specs=[pl.BlockSpec(memory_space=pl.ANY)] * len(panels),
        out_shape=[jax.ShapeDtypeStruct(shape, F32) for shape in shapes],
        scratch_shapes=[pltpu.SemaphoreType.DMA((len(panels),))],
        cost_estimate=CHEAP,
        compiler_params=pltpu.CompilerParams(vmem_limit_bytes=2**20),
    )(place, *hbm)


def column_of(row):
    shape = (row.shape[1], row.shape[1])
    same = lax.broadcasted_iota(jnp.int32, shape, 0) == lax.broadcasted_iota(jnp.int32, shape, 1)
    return jnp.sum(jnp.where(same, row, 0.0), axis=1, keepdims=True)


def edge_state_kernel(place, mine, other, pair_cols, cells, one, two, mass, weight, edge_ref, weight_ref):
    half = mine.shape[0]
    rows, width = one.shape
    for step, couple in enumerate((mine, other)):
        start = ((place[0] % 2) ^ step) * half
        edge_ref[pl.ds(pl.multiple_of(start, half), half), :] = exact_dot(couple[...], pair_cols[...])
    cell = column_of(cells[...].astype(F32))
    number = lax.broadcasted_iota(jnp.int32, (rows, width), 1)
    chosen = [(cell == (number + place[2 + side]).astype(F32)).astype(F32) for side in range(2)]
    picked = exact_dot(jnp.concatenate(chosen, axis=1), pair_cols[...])
    for index, value in enumerate((one[...], two[...], picked)):
        edge_ref[2 * half + index * rows:2 * half + (index + 1) * rows, :] = value
    edge_ref[2 * half + 3 * rows:, :] = jnp.broadcast_to(mass[...], (8, width))
    weight_ref[...] = weight[...]


def edge_call(rows, place, *values):
    vmem = pl.BlockSpec(memory_space=pltpu.VMEM)
    shapes = ((rows, values[2].shape[1]), values[-1].shape)
    return pl.pallas_call(
        edge_state_kernel,
        in_specs=[pl.BlockSpec(memory_space=pltpu.SMEM)] + [vmem] * len(values),
        out_specs=(vmem, vmem),
        out_shape=tuple(jax.ShapeDtypeStruct(shape, F32) for shape in shapes),
        cost_estimate=CHEAP,
        compiler_params=pltpu.CompilerParams(vmem_limit_bytes=6 * 2**20),
    )(place, *values)


def split_tall(place, pieces, high_ref, low_ref):
    width = high_ref.shape[1]
    blocks = 4 // len(pieces)
    for part, piece in enumerate(pieces):
        for block in range(blocks):
            number = block if len(pieces) == 1 else 2 * (place[1] ^ part) + block
            store_split(high_ref, low_ref, (number ^ place[0]) * width, piece, block * width, 0, width)


def tall_kernel(place, *refs):
    split_tall(place, refs[:-2], *refs[-2:])


def wide_kernel(place, *refs):
    pieces, (high_ref, low_ref) = refs[:-2], refs[-2:]
    width = high_ref.shape[1]
    blocks = 4 // len(pieces)
    for part, piece in enumerate(pieces):
        for block in range(blocks):
            number = block if len(pieces) == 1 else 2 * (place[1] ^ part) + block
            store_split(high_ref, low_ref, (number ^ place[0]) * width, piece, 0, block * width, width)


def edge_kernel(place, *refs):
    pieces, (high_ref, low_ref) = refs[:-2], refs[-2:]
    rows = pieces[0].shape[1] // 2
    for part, piece in enumerate(pieces):
        for bit in range(2):
            start = (bit ^ (place[0] % 2)) * 2 * rows + (place[1] ^ part) * rows
            store_split(high_ref, low_ref, start, piece, bit * rows, 0, rows)


def split_call(kernel, place, rows, *pieces):
    out = jax.ShapeDtypeStruct((rows, pieces[0].shape[1]), BF16)
    if kernel is wide_kernel:
        out = jax.ShapeDtypeStruct((rows, pieces[0].shape[0]), BF16)
    vmem = pl.BlockSpec(memory_space=pltpu.VMEM)
    return pl.pallas_call(
        kernel,
        in_specs=[pl.BlockSpec(memory_space=pltpu.SMEM)] + [vmem] * len(pieces),
        out_specs=(vmem, vmem),
        out_shape=(pltpu.VMEM(out.shape, BF16),) * 2,
        cost_estimate=CHEAP,
        compiler_params=pltpu.CompilerParams(vmem_limit_bytes=4 * 2**20),
    )(place, *pieces)


def product(left, high, low):
    rows = left.shape[0]
    left_high, left_low = halves_of(left)
    both = jnp.dot(jnp.concatenate([left_high, left_low], axis=0), high, preferred_element_type=F32)
    rest = jnp.dot(left_high, low, preferred_element_type=F32)
    return both[:rows] + both[rows:] + rest


def forward_half(one, picked, weights, edge):
    width = edge[0].shape[1]
    pairs = [one[:, side * 2 * width:(side + 1) * 2 * width] for side in range(2)]
    blocks = [product(pairs[tile // 2], edge[2 * tile][...], edge[2 * tile + 1][...]) for tile in range(4)]
    return jnp.concatenate(blocks, axis=1) + column_of(weights) * picked


def tall(left, panels):
    return jnp.concatenate([product(left, panels[2 * tile][...], panels[2 * tile + 1][...]) for tile in range(4)], axis=1)


def quad_sums(half, two, scale, lift):
    width = lift[0].shape[1]

    def column_block(block, part):
        return jnp.concatenate([lift[2 * tile + part][block * width:(block + 1) * width, :] for tile in range(4)], axis=0)

    sums = jnp.concatenate([product(half, column_block(block, 0), column_block(block, 1)) for block in range(4)], axis=1)
    return sums + two * scale


def below(tiles, rows, index, count):
    start = tiles[0].shape[1] + index * rows
    return jnp.concatenate([tile[start:start + count, :] for tile in tiles], axis=1)


def lead_kernel(s0, s1, s2, s3, weight, *refs):
    edge, lift, (half_ref, sums_ref) = refs[:8], refs[8:16], refs[16:]
    tiles, rows = (s0, s1, s2, s3), half_ref.shape[0]
    one, two, picked, scale = [below(tiles, rows, index, count) for index, count in enumerate((rows, rows, rows, 1))]
    half_ref[...] = forward_half(one, picked, weight[0:1, :], edge)
    sums_ref[...] = quad_sums(half_ref[...], two, scale, lift)


def root_kernel(sums, *refs):
    refs[-1][...] = tall(sums[...], refs[:-1])


def march_kernel(s0, s1, s2, s3, weight, half_start, two_start, place, *refs):
    edge, lift, root, back = refs[:8], refs[8:16], refs[16:24], refs[24:30]
    mine, other, one_ref, two_ref, last_high, last_low = refs[30:]
    rows, width = one_ref.shape
    tiles = (s0, s1, s2, s3)
    split_tall(place, (mine, other), last_high, last_low)
    back = back + (last_high, last_low)
    picked, scale = below(tiles, rows, 2, rows), below(tiles, rows, 3, 1)

    def advance(step, carry):
        half, two = carry
        half = forward_half(half - tall(two, back), picked, weight[pl.ds(step, 1), :], edge)
        return half, tall(quad_sums(half, two, scale, lift), root)

    half, two = lax.fori_loop(1, weight.shape[0], advance, (half_start[...], two_start[...]))
    one_ref[...] = half[:, :width] - product(two, back[0][...], back[1][...])
    two_ref[...] = two[:, :width]


def shards(
    adjoint_one_start,
    adjoint_two_start,
    couple_panel,
    pair_panel,
    lift_panel,
    root_panel,
    back_panel,
    mass_two,
    probe_cells,
    probe_weight,
):
    couple = couple_panel[0, 0]
    pair_cols = pair_panel[0, 0]
    lift = lift_panel[0, 0]
    root = root_panel[0, 0]
    back = back_panel[0, 0]
    width = couple.shape[0]
    rows = probe_cells.shape[0]
    column, row, core = lax.axis_index("gx"), lax.axis_index("gy"), lax.axis_index("gz")
    x_bit, y_bit = column % 2, row % 2
    first_cell = ((column - x_bit) * lax.axis_size("gy") + row) * width
    place = jnp.stack([2 * y_bit + x_bit, core, first_cell, first_cell + lax.axis_size("gy") * width]).astype(jnp.int32)

    couple_half, lift_half = cut_call(place, (couple, lift), ((width // 2, 2 * width), (width, 2 * width)))
    value = {"Cx": from_partner(couple_half, "gx"), "Ly": from_partner(lift_half, "gy"), "Lx": from_partner(lift_half, "gx")}
    back_half, root_half = cut_call(after(place, value["Cx"]), (back, root), ((2 * width, width),) * 2)
    own = {"L": lift_half, "B": back_half, "R": root_half}
    kernels = {"L": (wide_kernel, 4 * width), "R": (tall_kernel, 4 * width), "B": (tall_kernel, 4 * width), "E": (edge_kernel, 2 * width)}
    whole = after(place, lift_half)
    ready = {
        name: split_call(kernels[name][0], whole, kernels[name][1], panel)
        for name, panel in (("L", lift), ("R", root), ("B", back))
    }
    other = {}
    token = place
    for verb, name, *earlier in PLAN:
        kind, where = name[0], name[1:]
        if verb == "take":
            token = value[name] = after(value[name], token, *[ready[panel][0] for panel in earlier])
        elif verb == "edge":
            own["E"], weight = edge_call(
                width + 3 * rows + 8,
                place,
                couple_half,
                value["Cx"],
                pair_cols,
                probe_cells[None, :],
                adjoint_one_start[0, 0],
                adjoint_two_start[0, 0],
                mass_two[0],
                probe_weight,
            )
            value["E"] = own["E"]
        elif verb == "send":
            axis = where if where != "d" else "x" if kind in "EB" else "y"
            source = own[kind] if where != "d" else value[kind + ("y" if axis == "x" else "x")]
            value[name] = from_partner(after(source, token), "g" + axis)
        elif verb == "swap":
            other[name] = from_partner(after(value[name], token), "gz")
        elif verb == "lead":
            states = (own["E"], value["Ex"], value["Ey"], value["Ed"], weight)
            early = [panel for tile in ("E", "Ex", "Ey", "Ed", "L", "Lx", "Ly", "Ld") for panel in ready[tile]]
            ready[name] = pl.pallas_call(
                lead_kernel,
                in_specs=[pl.BlockSpec(memory_space=pltpu.VMEM)] * (5 + len(early)),
                out_specs=(pl.BlockSpec(memory_space=pltpu.VMEM),) * 2,
                out_shape=(jax.ShapeDtypeStruct((rows, 4 * width), F32),) * 2,
                cost_estimate=CHEAP,
                compiler_params=pltpu.CompilerParams(vmem_limit_bytes=6 * 2**20),
            )(*states, *early)
        elif verb == "root":
            roots = [panel for tile in ("R", "Rx", "Ry", "Rd") for panel in ready[tile]]
            two = pl.pallas_call(
                root_kernel,
                in_specs=[pl.BlockSpec(memory_space=pltpu.VMEM)] * (1 + len(roots)),
                out_specs=pl.BlockSpec(memory_space=pltpu.VMEM),
                out_shape=jax.ShapeDtypeStruct((rows, 4 * width), F32),
                cost_estimate=CHEAP,
                compiler_params=pltpu.CompilerParams(vmem_limit_bytes=6 * 2**20),
            )(ready["lead"][1], *roots)
        else:
            kernel, size = kernels[kind]
            ready[name] = split_call(kernel, after(place, token), size, value[name], other[name])

    vmem, smem = pl.BlockSpec(memory_space=pltpu.VMEM), pl.BlockSpec(memory_space=pltpu.SMEM)
    late = [panel for tile in ("B", "Bx", "By") for panel in ready[tile]] + [value["Bd"], other["Bd"]]
    one, two = pl.pallas_call(
        march_kernel,
        in_specs=[vmem] * 7 + [smem] + [vmem] * (len(early) + len(roots) + len(late)),
        out_specs=(vmem, vmem),
        out_shape=(jax.ShapeDtypeStruct((rows, width), F32),) * 2,
        scratch_shapes=[pltpu.VMEM((4 * width, width), BF16)] * 2,
        compiler_params=pltpu.CompilerParams(vmem_limit_bytes=12 * 2**20),
    )(*states, ready["lead"][0], two, place, *early, *roots, *late)
    return (one[None, None], two[None, None])


def solution(mesh):
    placed = (
        P(("groups", "gx"), "gy", "gz", None),
        P(("groups", "gx"), "gy", "gz", None),
        P(("groups", "gx"), "gy", None, None),
        P(("groups", "gx"), "gy", None, None),
        P(("groups", "gx"), "gy", None, None),
        P(("groups", "gx"), "gy", None, None),
        P(("groups", "gx"), "gy", None, None),
        P(("groups", "gx"), "gy", None),
        P(("groups", "gz")),
        P("groups", "gz"),
    )
    return jax.shard_map(
        shards,
        mesh=mesh,
        in_specs=placed,
        out_specs=(P(("groups", "gx"), "gy", "gz", None), P(("groups", "gx"), "gy", "gz", None)),
        check_vma=False,
    )
```

```python
import jax
import jax.numpy as jnp
from jax import lax
from jax.experimental import pallas as pl
from jax.experimental.pallas import tpu as pltpu
from jax.sharding import PartitionSpec as P

F32 = jnp.float32
BF16 = jnp.bfloat16


def from_partner(value, axis):
    pairs = [(source, source ^ 1) for source in range(lax.axis_size(axis))]
    return lax.ppermute(value, axis, pairs)


def after(value, *earlier):
    return lax.optimization_barrier((value,) + earlier)[0]


def exact_dot(left, right):
    return jnp.dot(left, right, precision=lax.Precision.HIGHEST, preferred_element_type=F32)


def halves_of(value):
    high = value.astype(BF16)
    return high, (value - high.astype(F32)).astype(BF16)


def store_split(high_ref, low_ref, start, piece, row, column, size):
    step = 32
    for offset in range(0, size, step):
        value = piece[row + offset:row + offset + step, column:column + high_ref.shape[1]]
        where = pl.ds(pl.multiple_of(start + offset, step), step)
        high_ref[where, :], low_ref[where, :] = halves_of(value)


PLAN = (
    ("take", "Cx"), ("send", "Rx"), ("send", "By"), ("edge", "E"),
    ("take", "Ly"), ("send", "Bx"), ("send", "Ey"),
    ("take", "Lx"), ("swap", "E"),
    ("take", "By", "L"), ("send", "Ry"), ("swap", "Ly"),
    ("take", "Rx", "R", "B"), ("send", "Ex"), ("swap", "Lx"), ("split", "E"),
    ("take", "Ey", "E"), ("send", "Ld"), ("split", "Ly"),
    ("take", "Bx", "Ly"), ("send", "Ed"), ("swap", "By"), ("swap", "Rx"), ("split", "By"), ("split", "Rx"),
    ("take", "Ry"), ("send", "Rd"), ("swap", "Ey"), ("split", "Lx"),
    ("take", "Ex", "Rx"), ("send", "Bd"),
    ("take", "Ld", "Lx"), ("swap", "Bx"), ("swap", "Ry"), ("swap", "Ex"), ("swap", "Ld"), ("split", "Ey"), ("split", "Ex"),
    ("take", "Ed", "By", "Ey"), ("swap", "Ed"), ("split", "Ld"),
    ("take", "Rd", "Ex"), ("swap", "Rd"), ("split", "Bx"), ("split", "Ed"), ("lead", "lead"),
    ("take", "Bd", "Ld", "Ed", "lead"), ("swap", "Bd"), ("split", "Ry"), ("split", "Rd"), ("root", "root"),
)


CHEAP = pl.CostEstimate(flops=1, transcendentals=0, bytes_accessed=1)


def cut_kernel(place, *refs):
    count = (len(refs) - 1) // 2
    panels, halves, sems = refs[:count], refs[count:2 * count], refs[-1]
    copies = []
    for index, (panel, half) in enumerate(zip(panels, halves)):
        rows, columns = half.shape
        if columns < panel.shape[1]:
            source = panel.at[:, pl.ds(pl.multiple_of(place[1] * columns, columns), columns)]
        else:
            source = panel.at[pl.ds(pl.multiple_of(place[1] * rows, rows), rows), :]
        copies.append(pltpu.make_async_copy(source, half, sems.at[index]))
    for copy in copies:
        copy.start()
    for copy in copies:
        copy.wait()


def cut_call(place, panels, shapes):
    hbm = [pltpu.with_memory_space_constraint(panel, pltpu.HBM) for panel in panels]
    return pl.pallas_call(
        cut_kernel,
        in_specs=[pl.BlockSpec(memory_space=pltpu.SMEM)] + [pl.BlockSpec(memory_space=pl.ANY)] * len(panels),
        out_specs=[pl.BlockSpec(memory_space=pl.ANY)] * len(panels),
        out_shape=[jax.ShapeDtypeStruct(shape, F32) for shape in shapes],
        scratch_shapes=[pltpu.SemaphoreType.DMA((len(panels),))],
        cost_estimate=CHEAP,
        compiler_params=pltpu.CompilerParams(vmem_limit_bytes=2**20),
    )(place, *hbm)


def column_of(row):
    shape = (row.shape[1], row.shape[1])
    same = lax.broadcasted_iota(jnp.int32, shape, 0) == lax.broadcasted_iota(jnp.int32, shape, 1)
    return jnp.sum(jnp.where(same, row, 0.0), axis=1, keepdims=True)


def edge_state_kernel(place, mine, other, pair_cols, cells, one, two, mass, weight, edge_ref, weight_ref):
    half = mine.shape[0]
    rows, width = one.shape
    for step, couple in enumerate((mine, other)):
        start = ((place[0] % 2) ^ step) * half
        edge_ref[pl.ds(pl.multiple_of(start, half), half), :] = exact_dot(couple[...], pair_cols[...])
    cell = column_of(cells[...].astype(F32))
    number = lax.broadcasted_iota(jnp.int32, (rows, width), 1)
    chosen = [(cell == (number + place[2 + side]).astype(F32)).astype(F32) for side in range(2)]
    picked = exact_dot(jnp.concatenate(chosen, axis=1), pair_cols[...])
    for index, value in enumerate((one[...], two[...], picked)):
        edge_ref[2 * half + index * rows:2 * half + (index + 1) * rows, :] = value
    edge_ref[2 * half + 3 * rows:, :] = jnp.broadcast_to(mass[...], (8, width))
    weight_ref[...] = weight[...]


def edge_call(rows, place, *values):
    vmem = pl.BlockSpec(memory_space=pltpu.VMEM)
    shapes = ((rows, values[2].shape[1]), values[-1].shape)
    return pl.pallas_call(
        edge_state_kernel,
        in_specs=[pl.BlockSpec(memory_space=pltpu.SMEM)] + [vmem] * len(values),
        out_specs=(vmem, vmem),
        out_shape=tuple(jax.ShapeDtypeStruct(shape, F32) for shape in shapes),
        cost_estimate=CHEAP,
        compiler_params=pltpu.CompilerParams(vmem_limit_bytes=6 * 2**20),
    )(place, *values)


def split_tall(place, pieces, high_ref, low_ref):
    width = high_ref.shape[1]
    blocks = 4 // len(pieces)
    for part, piece in enumerate(pieces):
        for block in range(blocks):
            number = block if len(pieces) == 1 else 2 * (place[1] ^ part) + block
            store_split(high_ref, low_ref, (number ^ place[0]) * width, piece, block * width, 0, width)


def tall_kernel(place, *refs):
    split_tall(place, refs[:-2], *refs[-2:])


def wide_kernel(place, *refs):
    pieces, (high_ref, low_ref) = refs[:-2], refs[-2:]
    width = high_ref.shape[1]
    blocks = 4 // len(pieces)
    for part, piece in enumerate(pieces):
        for block in range(blocks):
            number = block if len(pieces) == 1 else 2 * (place[1] ^ part) + block
            store_split(high_ref, low_ref, (number ^ place[0]) * width, piece, 0, block * width, width)


def edge_kernel(place, *refs):
    pieces, (high_ref, low_ref) = refs[:-2], refs[-2:]
    rows = pieces[0].shape[1] // 2
    for part, piece in enumerate(pieces):
        for bit in range(2):
            start = (bit ^ (place[0] % 2)) * 2 * rows + (place[1] ^ part) * rows
            store_split(high_ref, low_ref, start, piece, bit * rows, 0, rows)


def split_call(kernel, place, rows, *pieces):
    out = jax.ShapeDtypeStruct((rows, pieces[0].shape[1]), BF16)
    if kernel is wide_kernel:
        out = jax.ShapeDtypeStruct((rows, pieces[0].shape[0]), BF16)
    vmem = pl.BlockSpec(memory_space=pltpu.VMEM)
    return pl.pallas_call(
        kernel,
        in_specs=[pl.BlockSpec(memory_space=pltpu.SMEM)] + [vmem] * len(pieces),
        out_specs=(vmem, vmem),
        out_shape=(pltpu.VMEM(out.shape, BF16),) * 2,
        cost_estimate=CHEAP,
        compiler_params=pltpu.CompilerParams(vmem_limit_bytes=4 * 2**20),
    )(place, *pieces)


def product(left, high, low):
    rows = left.shape[0]
    left_high, left_low = halves_of(left)
    both = jnp.dot(jnp.concatenate([left_high, left_low], axis=0), high, preferred_element_type=F32)
    rest = jnp.dot(left_high, low, preferred_element_type=F32)
    return both[:rows] + both[rows:] + rest


def forward_half(one, picked, weights, edge):
    width = edge[0].shape[1]
    pairs = [one[:, side * 2 * width:(side + 1) * 2 * width] for side in range(2)]
    blocks = [product(pairs[tile // 2], edge[2 * tile][...], edge[2 * tile + 1][...]) for tile in range(4)]
    return jnp.concatenate(blocks, axis=1) + column_of(weights) * picked


def tall(left, panels):
    return jnp.concatenate([product(left, panels[2 * tile][...], panels[2 * tile + 1][...]) for tile in range(4)], axis=1)


def quad_sums(half, two, scale, lift):
    width = lift[0].shape[1]

    def column_block(block, part):
        return jnp.concatenate([lift[2 * tile + part][block * width:(block + 1) * width, :] for tile in range(4)], axis=0)

    sums = jnp.concatenate([product(half, column_block(block, 0), column_block(block, 1)) for block in range(4)], axis=1)
    return sums + two * scale


def below(tiles, rows, index, count):
    start = tiles[0].shape[1] + index * rows
    return jnp.concatenate([tile[start:start + count, :] for tile in tiles], axis=1)


def lead_kernel(s0, s1, s2, s3, weight, *refs):
    edge, lift, (half_ref, sums_ref) = refs[:8], refs[8:16], refs[16:]
    tiles, rows = (s0, s1, s2, s3), half_ref.shape[0]
    one, two, picked, scale = [below(tiles, rows, index, count) for index, count in enumerate((rows, rows, rows, 1))]
    half_ref[...] = forward_half(one, picked, weight[0:1, :], edge)
    sums_ref[...] = quad_sums(half_ref[...], two, scale, lift)


def root_kernel(sums, *refs):
    refs[-1][...] = tall(sums[...], refs[:-1])


def march_kernel(s0, s1, s2, s3, weight, half_start, two_start, place, *refs):
    edge, lift, root, back = refs[:8], refs[8:16], refs[16:24], refs[24:30]
    mine, other, one_ref, two_ref, last_high, last_low = refs[30:]
    rows, width = one_ref.shape
    tiles = (s0, s1, s2, s3)
    split_tall(place, (mine, other), last_high, last_low)
    back = back + (last_high, last_low)
    picked, scale = below(tiles, rows, 2, rows), below(tiles, rows, 3, 1)

    def advance(step, carry):
        half, two = carry
        half = forward_half(half - tall(two, back), picked, weight[pl.ds(step, 1), :], edge)
        return half, tall(quad_sums(half, two, scale, lift), root)

    half, two = lax.fori_loop(1, weight.shape[0], advance, (half_start[...], two_start[...]))
    one_ref[...] = half[:, :width] - product(two, back[0][...], back[1][...])
    two_ref[...] = two[:, :width]


def shards(
    adjoint_one_start,
    adjoint_two_start,
    couple_panel,
    pair_panel,
    lift_panel,
    root_panel,
    back_panel,
    mass_two,
    probe_cells,
    probe_weight,
):
    couple = couple_panel[0, 0]
    pair_cols = pair_panel[0, 0]
    lift = lift_panel[0, 0]
    root = root_panel[0, 0]
    back = back_panel[0, 0]
    width = couple.shape[0]
    rows = probe_cells.shape[0]
    column, row, core = lax.axis_index("gx"), lax.axis_index("gy"), lax.axis_index("gz")
    x_bit, y_bit = column % 2, row % 2
    first_cell = ((column - x_bit) * lax.axis_size("gy") + row) * width
    place = jnp.stack([2 * y_bit + x_bit, core, first_cell, first_cell + lax.axis_size("gy") * width]).astype(jnp.int32)

    couple_half, lift_half = cut_call(place, (couple, lift), ((width // 2, 2 * width), (width, 2 * width)))
    value = {"Cx": from_partner(couple_half, "gx"), "Ly": from_partner(lift_half, "gy"), "Lx": from_partner(lift_half, "gx")}
    back_half, root_half = cut_call(after(place, value["Cx"]), (back, root), ((2 * width, width),) * 2)
    own = {"L": lift_half, "B": back_half, "R": root_half}
    kernels = {"L": (wide_kernel, 4 * width), "R": (tall_kernel, 4 * width), "B": (tall_kernel, 4 * width), "E": (edge_kernel, 2 * width)}
    whole = after(place, lift_half)
    ready = {
        name: split_call(kernels[name][0], whole, kernels[name][1], panel)
        for name, panel in (("L", lift), ("R", root), ("B", back))
    }
    other = {}
    token = place
    for verb, name, *earlier in PLAN:
        kind, where = name[0], name[1:]
        if verb == "take":
            token = value[name] = after(value[name], token, *[ready[panel][0] for panel in earlier])
        elif verb == "edge":
            own["E"], weight = edge_call(
                width + 3 * rows + 8,
                place,
                couple_half,
                value["Cx"],
                pair_cols,
                probe_cells[None, :],
                adjoint_one_start[0, 0],
                adjoint_two_start[0, 0],
                mass_two[0],
                probe_weight,
            )
            value["E"] = own["E"]
        elif verb == "send":
            axis = where if where != "d" else "x" if kind in "EB" else "y"
            source = own[kind] if where != "d" else value[kind + ("y" if axis == "x" else "x")]
            value[name] = from_partner(after(source, token), "g" + axis)
        elif verb == "swap":
            other[name] = from_partner(after(value[name], token), "gz")
        elif verb == "lead":
            states = (own["E"], value["Ex"], value["Ey"], value["Ed"], weight)
            early = [panel for tile in ("E", "Ex", "Ey", "Ed", "L", "Lx", "Ly", "Ld") for panel in ready[tile]]
            ready[name] = pl.pallas_call(
                lead_kernel,
                in_specs=[pl.BlockSpec(memory_space=pltpu.VMEM)] * (5 + len(early)),
                out_specs=(pl.BlockSpec(memory_space=pltpu.VMEM),) * 2,
                out_shape=(jax.ShapeDtypeStruct((rows, 4 * width), F32),) * 2,
                cost_estimate=CHEAP,
                compiler_params=pltpu.CompilerParams(vmem_limit_bytes=6 * 2**20),
            )(*states, *early)
        elif verb == "root":
            roots = [panel for tile in ("R", "Rx", "Ry", "Rd") for panel in ready[tile]]
            two = pl.pallas_call(
                root_kernel,
                in_specs=[pl.BlockSpec(memory_space=pltpu.VMEM)] * (1 + len(roots)),
                out_specs=pl.BlockSpec(memory_space=pltpu.VMEM),
                out_shape=jax.ShapeDtypeStruct((rows, 4 * width), F32),
                cost_estimate=CHEAP,
                compiler_params=pltpu.CompilerParams(vmem_limit_bytes=6 * 2**20),
            )(ready["lead"][1], *roots)
        else:
            kernel, size = kernels[kind]
            ready[name] = split_call(kernel, after(place, token), size, value[name], other[name])

    vmem, smem = pl.BlockSpec(memory_space=pltpu.VMEM), pl.BlockSpec(memory_space=pltpu.SMEM)
    late = [panel for tile in ("B", "Bx", "By") for panel in ready[tile]] + [value["Bd"], other["Bd"]]
    one, two = pl.pallas_call(
        march_kernel,
        in_specs=[vmem] * 7 + [smem] + [vmem] * (len(early) + len(roots) + len(late)),
        out_specs=(vmem, vmem),
        out_shape=(jax.ShapeDtypeStruct((rows, width), F32),) * 2,
        scratch_shapes=[pltpu.VMEM((4 * width, width), BF16)] * 2,
        compiler_params=pltpu.CompilerParams(vmem_limit_bytes=12 * 2**20),
    )(*states, ready["lead"][0], two, place, *early, *roots, *late)
    return (one[None, None], two[None, None])


def solution(mesh):
    placed = (
        P(("groups", "gx"), "gy", "gz", None),
        P(("groups", "gx"), "gy", "gz", None),
        P(("groups", "gx"), "gy", None, None),
        P(("groups", "gx"), "gy", None, None),
        P(("groups", "gx"), "gy", None, None),
        P(("groups", "gx"), "gy", None, None),
        P(("groups", "gx"), "gy", None, None),
        P(("groups", "gx"), "gy", None),
        P(("groups", "gz")),
        P("groups", "gz"),
    )
    return jax.shard_map(
        shards,
        mesh=mesh,
        in_specs=placed,
        out_specs=(P(("groups", "gx"), "gy", "gz", None), P(("groups", "gx"), "gy", "gz", None)),
        check_vma=False,
    )
```
